32 devices in a mesh: row: 4 (over y, x), col: 8 (over z, core).
Axes of the slice: x: 2, y: 2, z: 4, core: 2. Of those that a mesh axis runs over, the one named last changes fastest.
Arguments:
- loads: float32 [4, 8, 1024, 8], P('row', 'col'), may hold values from -6 to 6
- schur: float32 [4, 8, 1024, 1024], P('row', 'col'), may hold values from -0.5 to 4.5, as said below
- factor: float32 [4, 8, 1024, 1024], P('row', 'col'), may hold values from -0.5 to 0.6, as said below
- coarse_inverse: float32 [1536, 1536], P(('row', 'col')), may hold values from -0.5 to 1.5, as said below
- elements: int32 [4, 8], P('row', 'col'), may hold values from 4096 to 16383
- west_map: int32 [4, 8, 256], P('row', 'col'), may hold values from 0 to 255, each once within a row
- south_map: int32 [4, 8, 256], P('row', 'col'), may hold values from 0 to 255, each once within a row
- prim_local: int32 [4, 8, 48], P('row', 'col'), may hold values from 0 to 1023
- prim_coarse: int32 [4, 8, 48], P('row', 'col'), may hold values from 0 to 1535
Outputs:
- solution: float32 [4, 8, 1024, 8], P('row', 'col')
- residual: float32 [4, 8, 1024, 8], P('row', 'col')
The draws below stay inside these ranges and needn't reach their ends.
Inputs may be any that keep to these rules, and one draw needn't show every extreme that they name: `schur`: symmetric positive definite. `factor`: symmetric positive definite. `coarse_inverse`: symmetric positive definite. `west_map`: each subdomain's row is a permutation of 0 to 255. `south_map`: each subdomain's row is a permutation of 0 to 255. `prim_local`: values may repeat. `prim_coarse`: values may repeat, within a subdomain and between subdomains.
All inputs are finite; a program needn't handle non-finite values.
Results may differ from the reference program's by a relative error of at most 0.0001.
Values sent between devices are 32-bit elements; how exact they have to be, the bound alone decides.
A program may use at most 128 MiB of HBM per device.

```python
import math
import jax
import jax.numpy as jnp
from jax import lax

NI = 1024
NPRIM = 48
NRHS = 8
ITERS = 1
ELEM_BASE = 4096
FACE = 256
NCO = 1536
N_ROW = 4
N_COL = 8


def symmetric_noise(key, leading, order):
    shape = leading + (order, order)
    base = jnp.clip(jax.random.normal(key, shape, jnp.float32), -6.0, 6.0)
    return (base + jnp.swapaxes(base, -1, -2)) / math.sqrt(2.0)


def schur_diagonal(key):
    spread = jax.random.uniform(jax.random.fold_in(key, 3), (N_ROW, N_COL, NI), jnp.float32)
    return 2.0 * jnp.exp(spread * math.log(2.0))


def draw_schur(key, part):
    diagonal = schur_diagonal(key)
    noise = symmetric_noise(jax.random.fold_in(key, 7), (N_ROW, N_COL), NI)
    return diagonal[..., None] * jnp.eye(NI, dtype=jnp.float32) + 0.5 / math.sqrt(NI) * noise


def draw_factor(key, part):
    diagonal = schur_diagonal(key)
    noise = symmetric_noise(jax.random.fold_in(key, 9), (N_ROW, N_COL), NI)
    return (1.0 / diagonal)[..., None] * jnp.eye(NI, dtype=jnp.float32) + 0.04 / math.sqrt(NI) * noise


def draw_coarse_inverse(key, part):
    diagonal = 0.5 + 0.5 * jax.random.uniform(jax.random.fold_in(key, 5), (NCO,), jnp.float32)
    noise = symmetric_noise(jax.random.fold_in(key, 13), (), NCO)
    return diagonal[:, None] * jnp.eye(NCO, dtype=jnp.float32) + 0.15 / math.sqrt(NCO) * noise


def with_ends(values, rng, smallest, high):
    longest = values.shape.index(max(values.shape))
    spots = []
    for shift in (0, 1):
        where = [jax.random.randint(jax.random.fold_in(rng, axis), (), 0, length) for axis, length in enumerate(values.shape)]
        where[longest] = (where[longest] + shift) % values.shape[longest]
        spots.append(tuple(where))
    return values.at[spots[0]].set(smallest).at[spots[1]].set(high)


def steps_of(own_key, shape, pieces, low, high):
    gain, own = 1.0, jax.random.fold_in(own_key, 6)
    for position, shards_of in pieces:
        draws = jnp.exp(jax.random.uniform(jax.random.fold_in(own, position), (shards_of,), jnp.float32, low / len(pieces), high / len(pieces)))
        gain = gain * jnp.repeat(draws, shape[position] // shards_of).reshape([-1 if axis == position else 1 for axis in range(len(shape))])
    return gain


def gaussian(rng, dims, scale, limit, pieces=(), held_as=jnp.bfloat16):
    values = scale * jax.random.normal(rng, dims, jnp.float32)
    if pieces:
        values = values * steps_of(rng, dims, pieces, -0.22, 0.18)
    return jnp.clip(values, -limit, limit).astype(held_as)


def setup_inputs(seed: int = 0) -> dict:
    seeds = jax.random.split(jax.random.key(seed), 10)
    return {
        "loads": gaussian(seeds[0], (N_ROW, N_COL, NI, NRHS), 1.0, 6.0, ((0, 4), (1, 8)), jnp.float32),
        "schur": draw_schur(jax.random.fold_in(seeds[9], 71), 0),
        "factor": draw_factor(jax.random.fold_in(seeds[9], 71), 0),
        "coarse_inverse": draw_coarse_inverse(jax.random.fold_in(seeds[9], 71), 0),
        "elements": with_ends(jax.random.randint(seeds[4], (N_ROW, N_COL), ELEM_BASE, 4 * ELEM_BASE), jax.random.fold_in(seeds[4], 1), ELEM_BASE, (4 * ELEM_BASE) - 1).astype(jnp.int32),
        "west_map": jax.vmap(lambda own: jax.random.permutation(own, FACE))(jax.random.split(seeds[5], N_ROW * N_COL)).reshape((N_ROW, N_COL, FACE)).astype(jnp.int32),
        "south_map": jax.vmap(lambda own: jax.random.permutation(own, FACE))(jax.random.split(seeds[6], N_ROW * N_COL)).reshape((N_ROW, N_COL, FACE)).astype(jnp.int32),
        "prim_local": with_ends(jax.random.randint(seeds[7], (N_ROW, N_COL, NPRIM), 0, NI), jax.random.fold_in(seeds[7], 1), 0, NI - 1).astype(jnp.int32),
        "prim_coarse": with_ends(jax.random.randint(seeds[8], (N_ROW, N_COL, NPRIM), 0, NCO), jax.random.fold_in(seeds[8], 1), 0, NCO - 1).astype(jnp.int32),
    }


HIGHEST_PRECISION = lax.Precision.HIGHEST


def face_weights():
    face_ids = jnp.arange(NI) // FACE
    column_ids = jnp.arange(N_COL)
    row_ids = jnp.arange(N_ROW)
    neighbour_flags = jnp.stack([
        jnp.broadcast_to(column_ids[None, :] > 0, (N_ROW, N_COL)),
        jnp.broadcast_to(column_ids[None, :] < N_COL - 1, (N_ROW, N_COL)),
        jnp.broadcast_to(row_ids[:, None] > 0, (N_ROW, N_COL)),
        jnp.broadcast_to(row_ids[:, None] < N_ROW - 1, (N_ROW, N_COL))], axis=-1)
    return jnp.where(neighbour_flags[:, :, face_ids], 0.5, 1.0).astype(jnp.float32)[..., None]


def pick_rows(values, orders):
    return jax.vmap(jax.vmap(lambda source, places: jnp.take(source, places, axis=0)))(values, orders)


def place_rows(values, orders):
    return jax.vmap(jax.vmap(lambda source, places: jnp.zeros_like(source).at[places].set(source)))(values, orders)


def assemble(values, west_map, south_map):
    west_face = values[:, :, :FACE]
    east_face = values[:, :, FACE:2 * FACE]
    south_face = values[:, :, 2 * FACE:3 * FACE]
    north_face = values[:, :, 3 * FACE:]
    blank_column = jnp.zeros((N_ROW, 1, FACE, NRHS), jnp.float32)
    blank_row = jnp.zeros((1, N_COL, FACE, NRHS), jnp.float32)
    from_west = jnp.concatenate([blank_column, east_face[:, :-1]], axis=1)
    west_add = pick_rows(from_west, west_map)
    from_east = jnp.concatenate([place_rows(west_face, west_map)[:, 1:], blank_column], axis=1)
    from_south = jnp.concatenate([blank_row, north_face[:-1]], axis=0)
    south_add = pick_rows(from_south, south_map)
    from_north = jnp.concatenate([place_rows(south_face, south_map)[1:], blank_row], axis=0)
    return values + jnp.concatenate([west_add, from_east, south_add, from_north], axis=2)


def local_solve(operands):
    schur_block, factor_block, scaled, sweeps = operands
    first = jnp.dot(factor_block, scaled, precision=HIGHEST_PRECISION, preferred_element_type=jnp.float32)

    def sweep(turn, current):
        inner_term = jnp.dot(schur_block, current, precision=HIGHEST_PRECISION, preferred_element_type=jnp.float32)
        return current + jnp.dot(factor_block, scaled - inner_term, precision=HIGHEST_PRECISION, preferred_element_type=jnp.float32)

    return lax.fori_loop(1, sweeps, sweep, first)


def coarse_part(scaled, prim_local, prim_coarse, coarse_inverse):
    picked = pick_rows(scaled, prim_local)
    right_side = jnp.zeros((NCO, NRHS), jnp.float32).at[prim_coarse.reshape(-1)].add(picked.reshape(-1, NRHS))
    solved = jnp.dot(coarse_inverse, right_side, precision=HIGHEST_PRECISION, preferred_element_type=jnp.float32)
    spread = jnp.take(solved, prim_coarse.reshape(-1), axis=0).reshape(N_ROW, N_COL, NPRIM, NRHS)
    return jax.vmap(jax.vmap(lambda source, places: jnp.zeros((NI, NRHS), jnp.float32).at[places].add(source)))(spread, prim_local)


def reference(loads, schur, factor, coarse_inverse, elements, west_map, south_map, prim_local, prim_coarse):
    weights = face_weights()
    sweep_count = elements // ELEM_BASE

    def operator(values):
        return assemble(jnp.matmul(schur, values, precision=HIGHEST_PRECISION), west_map, south_map)

    def precondition(current):
        scaled = weights * current
        local = lax.map(local_solve, (schur.reshape(-1, NI, NI), factor.reshape(-1, NI, NI),
                                      scaled.reshape(-1, NI, NRHS), sweep_count.reshape(-1)))
        local = local.reshape(N_ROW, N_COL, NI, NRHS)
        correction = coarse_part(scaled, prim_local, prim_coarse, coarse_inverse)
        return assemble(weights * (local + correction), west_map, south_map)

    def inner(first, second):
        return jnp.sum(weights * first * second, axis=(0, 1, 2))

    right_side = assemble(loads, west_map, south_map)
    solution = jnp.zeros_like(right_side)
    residual = right_side
    precond = precondition(residual)
    direction = precond
    product_now = inner(residual, precond)
    for iteration in range(ITERS):
        image = operator(direction)
        alpha = product_now / inner(direction, image)
        solution = solution + alpha * direction
        residual = residual - alpha * image
        if iteration + 1 < ITERS:
            precond = precondition(residual)
            product_next = inner(residual, precond)
            direction = precond + (product_next / product_now) * direction
            product_now = product_next
    return solution, residual
```

```python
import functools

import jax
import jax.numpy as jnp
from jax import lax
from jax.experimental import pallas as pl
from jax.experimental.pallas import tpu as pltpu
from jax.sharding import PartitionSpec as P

ELEM_BASE = 4096
MOST_SWEEPS = 3
MESH = pl.DeviceIdType.MESH
F32, BF16 = jnp.float32, jnp.bfloat16
NT = (((1,), (1,)), ((), ()))
IDX, RHS, SOL, SUM = range(4)


def split(values):
    high = values.astype(BF16).astype(F32)
    return jnp.concatenate([high, values - high], axis=0).astype(BF16)


def join(stacked):
    rows = stacked.shape[0] // 2
    return stacked[:rows] + stacked[rows:]


def one_hot(numbers, wanted):
    return jnp.where(numbers == wanted, 1.0, 0.0).astype(BF16)


def dot(a, b):
    return jnp.dot(a, b, preferred_element_type=F32)


def dot_nt(a, b):
    return lax.dot_general(a, b, NT, preferred_element_type=F32)


def kernel(
    n_row, n_col, loads_hbm, schur_hbm, factor_hbm, coarse_hbm, elements_hbm, west_hbm, south_hbm,
    local_hbm, prim_hbm, direction, image_out, loads_out, alpha_out,
    loads, elements, west_map, south_map, prim_local, prim_coarse, schur_in, factor_in, coarse_in, schur_hi, schur_lo, factor_hi, factor_lo,
    coarse_split, columns, west_hot, south_hot, local_hot, coarse_hot,
    place, idx_all, val_all, sum_all, face_out, face_in,
    copy_sem, face_send, face_recv, all_send, all_recv,
):
    a, c = lax.axis_index("row"), lax.axis_index("col")
    unknowns = loads.shape[1]
    face = unknowns // 4
    wide = local_hot.shape[1]
    half = wide // 2
    count = n_row * n_col
    me = a * n_col + c
    odd = lax.rem(me, 2)
    coarse_rows, coarse_all = coarse_in.shape
    nprim = prim_local.shape[1]

    copies = [
        pltpu.make_async_copy(src, dst, copy_sem.at[i])
        for i, (src, dst) in enumerate(
            [
                (factor_hbm, factor_in), (coarse_hbm, coarse_in), (schur_hbm, schur_in),
                (loads_hbm, loads), (west_hbm, west_map), (south_hbm, south_map),
                (local_hbm, prim_local), (prim_hbm, prim_coarse), (elements_hbm, elements),
            ]
        )
    ]
    barrier = pltpu.get_barrier_semaphore()
    def peer(d):
        other = lax.rem(me + d, count)
        return (lax.div(other, n_col), lax.rem(other, n_col))

    def each(work):
        if count <= 64:
            for d in range(1, count):
                work(d)
        else:
            lax.fori_loop(1, count, lambda d, carry: (work(d), carry)[1], 0)

    each(lambda d: pl.semaphore_signal(barrier, inc=1, device_id=peer(d), device_id_type=MESH))
    for copy in copies[3:] + copies[:3]:
        copy.start()
    for copy in copies[3:]:
        copy.wait()

    def hot(order_ref):
        return one_hot(lax.broadcasted_iota(jnp.int32, (face, face), 0), order_ref[...])

    west_hot[...] = hot(west_map)
    south_hot[...] = hot(south_map)

    def placed(source):
        place[...] = jnp.full(place.shape, -1, jnp.int32)
        place[:1, :nprim] = source[...]
        base = place[...]
        return base, pltpu.roll(base, half, 1)

    base, rolled = placed(prim_coarse)
    own_coarse = jnp.where(odd == 1, rolled, base)[:1]
    own_local = jnp.maximum(*placed(prim_local))[:1]
    idx_all[me] = own_coarse

    lane = lax.broadcasted_iota(jnp.int32, (1, unknowns), 1)
    flags = [c > 0, c < n_col - 1, a > 0, a < n_row - 1]
    halves = [jnp.where(flag, 0.5, 1.0).astype(F32) for flag in flags]
    weights = jnp.where(
        lane < face,
        halves[0],
        jnp.where(lane < 2 * face, halves[1], jnp.where(lane < 3 * face, halves[2], halves[3])),
    )
    targets = [(a, c + 1), (a, c - 1), (a + 1, c), (a - 1, c)]
    can_send = [flags[1], flags[0], flags[3], flags[2]]

    def face_copy(turn, slot):
        return pltpu.make_async_remote_copy(
            src_ref=face_out.at[turn, slot],
            dst_ref=face_in.at[turn, slot],
            send_sem=face_send.at[turn, slot],
            recv_sem=face_recv.at[turn, slot],
            device_id=targets[slot],
            device_id_type=MESH,
        )

    def face_fill(turn, values):
        face_out[turn, 0] = values[:, face : 2 * face]
        face_out[turn, 2] = values[:, 3 * face :]
        face_out[turn, 1] = join(dot_nt(split(values[:, :face]), west_hot[...]))
        face_out[turn, 3] = join(dot_nt(split(values[:, 2 * face : 3 * face]), south_hot[...]))

    def face_start(turn):
        for slot in range(4):
            @pl.when(can_send[slot])
            def _():
                face_copy(turn, slot).start()

    def face_finish(turn, values):
        for slot in range(4):
            @pl.when(flags[slot])
            def _():
                face_copy(turn, slot).wait_recv()

            @pl.when(jnp.logical_not(flags[slot]))
            def _():
                face_in[turn, slot] = jnp.zeros(face_in.shape[2:], F32)
        adds = [
            join(dot(split(face_in[turn, 0]), west_hot[...])),
            face_in[turn, 1],
            join(dot(split(face_in[turn, 2]), south_hot[...])),
            face_in[turn, 3],
        ]
        return values + jnp.concatenate(adds, axis=1)

    def all_copy(buffer, kind, d):
        return pltpu.make_async_remote_copy(
            src_ref=buffer.at[me],
            dst_ref=buffer.at[me],
            send_sem=all_send.at[kind, d],
            recv_sem=all_recv.at[kind, d],
            device_id=peer(d),
            device_id_type=MESH,
        )

    def start(buffer, kind):
        each(lambda d: all_copy(buffer, kind, d).start())

    def arrive(buffer, kind):
        each(lambda d: all_copy(buffer, kind, d).wait_recv())

    rhs = loads.shape[0]
    lower = lax.broadcasted_iota(jnp.int32, (rhs // 2, wide), 1) < half

    def pack(values):
        return jnp.where(lower, values[: rhs // 2], values[rhs // 2 :])

    def unpack(first, second):
        both = jnp.concatenate([first, second], axis=0)
        swapped = pltpu.roll(both, half, 1)
        top = jnp.where(lower, both[: rhs // 2], swapped[rhs // 2 :])
        bottom = jnp.where(lower, swapped[: rhs // 2], both[rhs // 2 :])
        return jnp.concatenate([top, bottom], axis=0)

    first = loads[...]
    face_fill(0, first)
    pl.semaphore_wait(barrier, count - 1)
    face_start(0)
    start(idx_all, IDX)

    rows_iota = lax.broadcasted_iota(jnp.int32, (unknowns, wide), 0)
    local_hot[...] = one_hot(rows_iota, own_local)

    def split_matrix(source, high, low):
        step = 128

        def one(i, carry):
            at = pl.ds(pl.multiple_of(i * step, step), step)
            values = source[at, :]
            top = values.astype(BF16)
            high[at, :] = top
            low[at, :] = (values - top.astype(F32)).astype(BF16)
            return carry

        lax.fori_loop(0, source.shape[0] // step, one, 0)

    copies[0].wait()
    split_matrix(factor_in, factor_hi, factor_lo)

    right_side = face_finish(0, first)
    scaled = weights * right_side
    val_all[0, me] = pack(join(dot(split(scaled), local_hot[...])))
    start(val_all.at[0], RHS)

    def apply(high, low, vectors):
        both = split(vectors)
        return join(dot(both, high[...]) + dot(both, low[...]))

    local = apply(factor_hi, factor_lo, scaled)

    copies[1].wait()
    values = coarse_in[...]
    top = values.astype(BF16)
    coarse_split[...] = jnp.zeros(coarse_split.shape, BF16)
    coarse_split[:coarse_rows, :] = top
    coarse_split[half : half + coarse_rows, :] = (values - top.astype(F32)).astype(BF16)
    arrive(idx_all, IDX)
    chunk = 256
    chunks = coarse_all // chunk
    small = lax.broadcasted_iota(jnp.int32, (chunk, 2 * wide), 0).astype(F32).astype(BF16)

    def one_column(s, carry):
        wanted = jnp.concatenate(
            [jnp.maximum(idx_all[4 * s + i], idx_all[4 * s + i + 1]) for i in (0, 2)], axis=1
        )

        def one_chunk(k, acc):
            start_at = k * chunk
            offset = wanted - start_at
            inside = jnp.logical_and(offset >= 0, offset < chunk)
            offset = jnp.where(inside, offset, -1).astype(F32).astype(BF16)
            picks = jnp.where(small == offset, jnp.ones_like(small), jnp.zeros_like(small))
            return acc + dot(coarse_split[:, pl.ds(start_at, chunk)], picks)

        acc = jnp.zeros((wide, 2 * wide), F32)
        if chunks <= 8:
            for k in range(chunks):
                acc = one_chunk(k, acc)
        else:
            acc = lax.fori_loop(
                0, chunks, lambda k, acc: one_chunk(pl.multiple_of(k, 1), acc), acc
            )
        values = join(acc)
        top = values.astype(BF16)
        at = pl.ds(pl.multiple_of(s * 2 * wide, 2 * wide), 2 * wide)
        columns[:half, at] = top
        columns[half:, at] = (values - top.astype(F32)).astype(BF16)
        return carry

    lax.fori_loop(0, count // 4, one_column, 0)

    def gathered(buffer):
        return split(
            jnp.concatenate([unpack(buffer[s], buffer[s + 1]) for s in range(0, count, 2)], axis=1)
        )

    arrive(val_all.at[0], RHS)
    solved = join(dot_nt(gathered(val_all.at[0]), columns[...]))
    solved = solved + pltpu.roll(solved, half, 1)
    val_all[1, me] = pack(solved)
    start(val_all.at[1], SOL)

    copies[2].wait()
    split_matrix(schur_in, schur_hi, schur_lo)

    at = lax.broadcasted_iota(jnp.int32, (wide, wide), 0)
    upper = (at >= half).astype(jnp.int32)
    number = upper * coarse_rows + at - upper * half
    number = jnp.where(at - upper * half < coarse_rows, number, -2 * coarse_all)

    def one_pick(s, carry):
        coarse_hot[pl.ds(pl.multiple_of(s * wide, wide), wide), :] = one_hot(
            number, own_coarse - s * 2 * coarse_rows
        )
        return carry

    lax.fori_loop(0, count // 2, one_pick, 0)

    for turn in range(2, MOST_SWEEPS + 1):
        inner = scaled - apply(schur_hi, schur_lo, local)
        later = local + apply(factor_hi, factor_lo, inner)
        more = jnp.broadcast_to(elements[...], local.shape) >= turn * ELEM_BASE
        local = jnp.where(more, later, local)

    arrive(val_all.at[1], SOL)
    read = join(dot(gathered(val_all.at[1]), coarse_hot[...]))
    correction = join(dot_nt(split(read), local_hot[...]))
    halved = weights * (local + correction)
    face_fill(1, halved)
    face_start(1)

    def lane_sum(values):
        return jnp.sum(values, axis=1, keepdims=True)

    rz = lane_sum(right_side * halved)
    precond = face_finish(1, halved)
    image = apply(schur_hi, schur_lo, precond)
    pq = lane_sum(precond * image)
    sum_lane = lax.broadcasted_iota(jnp.int32, (rhs, 128), 1)
    sum_case = lax.broadcasted_iota(jnp.int32, (rhs, 128), 0)
    upper_lane, lower_lane = sum_lane == sum_case + rhs, sum_lane == sum_case
    laid = jnp.where(lower_lane, rz, 0.0) + jnp.where(upper_lane, pq, 0.0)
    sum_all[me] = jnp.sum(laid, axis=0, keepdims=True)
    start(sum_all, SUM)
    face_fill(2, image)
    face_start(2)
    direction[...] = precond
    loads_out[...] = right_side
    image_out[...] = face_finish(2, image)
    arrive(sum_all, SUM)
    sums = sum_all[0]
    for i in range(1, count):
        sums = sums + sum_all[i]
    sums = jnp.broadcast_to(sums, (rhs, 128))
    alpha = lane_sum(jnp.where(lower_lane, sums, 0.0)) / lane_sum(jnp.where(upper_lane, sums, 0.0))
    alpha_out[...] = jnp.broadcast_to(alpha, alpha_out.shape)

    for kind, buffer in enumerate([idx_all, val_all.at[0], val_all.at[1], sum_all]):
        each(lambda d: all_copy(buffer, kind, d).wait_send())
    for turn in range(3):
        for slot in range(4):
            @pl.when(can_send[slot])
            def _():
                face_copy(turn, slot).wait_send()


def up(n, to):
    return -(-n // to) * to


def body(
    n_row, n_col, loads, schur, factor, coarse_inverse, elements, west_map, south_map,
    prim_local, prim_coarse,
):
    vectors = loads[0, 0].T
    rhs, unknowns = vectors.shape
    face = unknowns // 4
    coarse_rows, coarse_all = coarse_inverse.shape
    nprim = prim_local.shape[2]
    wide = 2 * up(max(nprim, coarse_rows), 64)
    count = n_row * n_col
    vmem = pl.BlockSpec(memory_space=pltpu.VMEM)
    hbm = pl.BlockSpec(memory_space=pl.ANY)
    dma = pltpu.SemaphoreType.DMA
    out = pltpu.VMEM(vectors.shape, F32)
    direction, image, right_side, alpha = pl.pallas_call(
        functools.partial(kernel, n_row, n_col),
        out_shape=(out, out, out, out),
        in_specs=[hbm] * 9,
        out_specs=(vmem, vmem, vmem, vmem),
        scratch_shapes=[
            pltpu.VMEM(vectors.shape, F32),
            pltpu.VMEM((1, 1), jnp.int32),
            pltpu.VMEM((1, face), jnp.int32),
            pltpu.VMEM((1, face), jnp.int32),
            pltpu.VMEM((1, nprim), jnp.int32),
            pltpu.VMEM((1, nprim), jnp.int32),
            pltpu.VMEM((unknowns, unknowns), F32),
            pltpu.VMEM((unknowns, unknowns), F32),
            pltpu.VMEM((coarse_rows, coarse_all), F32),
            pltpu.VMEM((unknowns, unknowns), BF16),
            pltpu.VMEM((unknowns, unknowns), BF16),
            pltpu.VMEM((unknowns, unknowns), BF16),
            pltpu.VMEM((unknowns, unknowns), BF16),
            pltpu.VMEM((wide, coarse_all), BF16),
            pltpu.VMEM((wide, count // 2 * wide), BF16),
            pltpu.VMEM((face, face), BF16),
            pltpu.VMEM((face, face), BF16),
            pltpu.VMEM((unknowns, wide), BF16),
            pltpu.VMEM((count // 2 * wide, wide), BF16),
            pltpu.VMEM((8, wide), jnp.int32),
            pltpu.VMEM((count, 1, wide), jnp.int32),
            pltpu.VMEM((2, count, rhs // 2, wide), F32),
            pltpu.VMEM((count, 1, 128), F32),
            pltpu.VMEM((3, 4, rhs, face), F32),
            pltpu.VMEM((3, 4, rhs, face), F32),
            dma((9,)),
            dma((3, 4)),
            dma((3, 4)),
            dma((4, count)),
            dma((4, count)),
        ],
        compiler_params=pltpu.CompilerParams(collective_id=0, has_side_effects=True),
    )(
        vectors, schur[0, 0], factor[0, 0], coarse_inverse, elements,
        west_map[0], south_map[0], prim_local[0], prim_coarse[0],
    )
    solution = alpha * direction
    residual = right_side - alpha * image
    return solution.T[None, None], residual.T[None, None]


def solution(mesh):
    placed = (
        P("row", "col", None, None),
        P("row", "col", None, None),
        P("row", "col", None, None),
        P(("row", "col"), None),
        P("row", "col"),
        P("row", "col", None),
        P("row", "col", None),
        P("row", "col", None),
        P("row", "col", None),
    )
    return jax.shard_map(
        functools.partial(body, mesh.shape["row"], mesh.shape["col"]),
        mesh=mesh,
        in_specs=placed,
        out_specs=(P("row", "col", None, None), P("row", "col", None, None)),
        check_vma=False,
    )
```

```python
import functools

import jax
import jax.numpy as jnp
from jax import lax
from jax.experimental import pallas as pl
from jax.experimental.pallas import tpu as pltpu
from jax.sharding import PartitionSpec as P

ELEM_BASE = 4096
MOST_SWEEPS = 3
MESH = pl.DeviceIdType.MESH
F32, BF16 = jnp.float32, jnp.bfloat16
NT = (((1,), (1,)), ((), ()))
IDX, RHS, SOL, SUM = range(4)


def split(values):
    high = values.astype(BF16).astype(F32)
    return jnp.concatenate([high, values - high], axis=0).astype(BF16)


def join(stacked):
    rows = stacked.shape[0] // 2
    return stacked[:rows] + stacked[rows:]


def one_hot(numbers, wanted):
    return jnp.where(numbers == wanted, 1.0, 0.0).astype(BF16)


def dot(a, b):
    return jnp.dot(a, b, preferred_element_type=F32)


def dot_nt(a, b):
    return lax.dot_general(a, b, NT, preferred_element_type=F32)


def flip(value, mask, size):
    out, weight = 0, 1
    while weight < size:
        bit = lax.rem(lax.div(value, weight), 2)
        if isinstance(mask, int):
            bit = 1 - bit if (mask // weight) % 2 else bit
        else:
            bit = lax.rem(bit + lax.rem(lax.div(mask, weight), 2), 2)
        out, weight = out + weight * bit, 2 * weight
    return out


def kernel(
    n_row, n_col, loads_hbm, schur_hbm, factor_hbm, coarse_hbm, elements_hbm, west_hbm, south_hbm,
    local_hbm, prim_hbm, direction, image_out, loads_out, alpha_out,
    loads, elements, west_map, south_map, prim_local, prim_coarse,
    schur_in, factor_in, coarse_in, schur_hi, schur_lo, factor_hi, factor_lo,
    coarse_split, columns, west_hot, south_hot, local_hot, coarse_hot, place_hot,
    place, wide_place, idx_all, val_all, sum_all, face_out, face_in, near_out, near_in,
    copy_sem, face_send, face_recv, near_send, near_recv, all_send, all_recv, entered,
):
    a, c = lax.axis_index("row"), lax.axis_index("col")
    unknowns = loads.shape[1]
    face = unknowns // 4
    wide = local_hot.shape[1]
    half = wide // 2
    count = n_row * n_col
    me = a * n_col + c
    odd = lax.rem(me, 2)
    coarse_rows, coarse_all = coarse_in.shape
    nprim = prim_local.shape[1]
    lanes = near_out.shape[1]
    five = place_hot.shape[1]

    copies = [
        pltpu.make_async_copy(src, dst, copy_sem.at[i])
        for i, (src, dst) in enumerate(
            [
                (factor_hbm, factor_in), (coarse_hbm, coarse_in), (schur_hbm, schur_in),
                (loads_hbm, loads), (west_hbm, west_map), (south_hbm, south_map),
                (local_hbm, prim_local), (prim_hbm, prim_coarse), (elements_hbm, elements),
            ]
        )
    ]
    barrier = pltpu.get_barrier_semaphore()
    column_mates = [(flip(a, m, n_row), c) for m in range(1, n_row)]
    row_mates = [(a, flip(c, m, n_col)) for m in range(1, n_col)]
    for mate in row_mates + column_mates:
        pl.semaphore_signal(barrier, inc=1, device_id=mate, device_id_type=MESH)
    for copy in copies[3:] + copies[:3]:
        copy.start()

    rows_of, cols_of = {}, {}

    def peer(m):
        if not isinstance(m, int):
            return (flip(a, lax.div(m, n_col), n_row), flip(c, lax.rem(m, n_col), n_col))
        row, col = m // n_col, m % n_col
        if row not in rows_of:
            rows_of[row] = flip(a, row, n_row)
        if col not in cols_of:
            cols_of[col] = flip(c, col, n_col)
        return (rows_of[row], cols_of[col])

    def each(work):
        if count <= 64:
            for m in range(count - 1, 0, -1):
                work(m)
        else:
            lax.fori_loop(1, count, lambda d, carry: (work(count - d), carry)[1], 0)

    for copy in copies[3:]:
        copy.wait()

    def hot(order_ref):
        return one_hot(lax.broadcasted_iota(jnp.int32, (face, face), 0), order_ref[...])

    west_hot[...] = hot(west_map)
    south_hot[...] = hot(south_map)

    lane = lax.broadcasted_iota(jnp.int32, (1, unknowns), 1)
    flags = [c > 0, c < n_col - 1, a > 0, a < n_row - 1]
    halves = [jnp.where(flag, 0.5, 1.0).astype(F32) for flag in flags]
    weights = jnp.where(
        lane < face,
        halves[0],
        jnp.where(lane < 2 * face, halves[1], jnp.where(lane < 3 * face, halves[2], halves[3])),
    )
    targets = [(a, c + 1), (a, c - 1), (a + 1, c), (a - 1, c)]
    can_send = [flags[1], flags[0], flags[3], flags[2]]

    def face_copy(turn, slot):
        return pltpu.make_async_remote_copy(
            src_ref=face_out.at[turn, slot],
            dst_ref=face_in.at[turn, slot],
            send_sem=face_send.at[turn, slot],
            recv_sem=face_recv.at[turn, slot],
            device_id=targets[slot],
            device_id_type=MESH,
        )

    def near_copy(slot):
        return pltpu.make_async_remote_copy(
            src_ref=near_out,
            dst_ref=near_in.at[slot],
            send_sem=near_send.at[slot],
            recv_sem=near_recv.at[slot],
            device_id=targets[slot],
            device_id_type=MESH,
        )

    def face_fill(turn, values):
        face_out[turn, 0] = values[:, face : 2 * face]
        face_out[turn, 2] = values[:, 3 * face :]
        face_out[turn, 1] = join(dot_nt(split(values[:, :face]), west_hot[...]))
        face_out[turn, 3] = join(dot_nt(split(values[:, 2 * face : 3 * face]), south_hot[...]))

    def when_neighbour(present, work):
        for slot in range(4):
            @pl.when(present[slot])
            def _():
                work(slot)

    def face_finish(turn, values):
        for slot in range(4):
            @pl.when(flags[slot])
            def _():
                face_copy(turn, slot).wait_recv()

            @pl.when(jnp.logical_not(flags[slot]))
            def _():
                face_in[turn, slot] = jnp.zeros(face_in.shape[2:], F32)
        adds = [
            join(dot(split(face_in[turn, 0]), west_hot[...])),
            face_in[turn, 1],
            join(dot(split(face_in[turn, 2]), south_hot[...])),
            face_in[turn, 3],
        ]
        return values + jnp.concatenate(adds, axis=1)

    first = loads[...]
    face_fill(0, first)
    pl.semaphore_wait(barrier, n_row + n_col - 2)
    when_neighbour(can_send, lambda slot: face_copy(0, slot).start())
    for mate in column_mates:
        pl.semaphore_signal(entered, inc=1, device_id=mate, device_id_type=MESH)

    def placed(source):
        place[...] = jnp.full(place.shape, -1, jnp.int32)
        place[:1, :nprim] = source[...]
        base = place[...]
        return base, pltpu.roll(base, half, 1)

    base, rolled = placed(prim_coarse)
    own_coarse = jnp.where(odd == 1, rolled, base)[:1]
    idx_all[me] = own_coarse
    near_out[...] = jnp.full(near_out.shape, -1, jnp.int32)
    near_out[:1, :nprim] = prim_coarse[...]
    near_out[1:2, :nprim] = prim_local[...]
    numbers = near_out[1:2, :]
    depth = lax.broadcasted_iota(jnp.int32, (face, lanes), 0)

    def look_up(table, numbers, offset):
        inside = jnp.logical_and(numbers >= 0, numbers < face)
        table = jnp.broadcast_to(table, (8, face)).astype(F32)
        found = join(dot(split(table), one_hot(depth, numbers)))[:1]
        return jnp.where(inside, found.astype(jnp.int32) + offset, -1)

    near_out[2:3, :] = look_up(west_map[...], numbers, face)
    near_out[3:4, :] = look_up(south_map[...], numbers - 2 * face, 3 * face)
    when_neighbour(can_send, lambda slot: near_copy(slot).start())

    own_local = jnp.maximum(*placed(prim_local))[:1]
    rows_iota = lax.broadcasted_iota(jnp.int32, (unknowns, wide), 0)
    local_hot[...] = one_hot(rows_iota, own_local)

    def all_copy(buffer, kind, m):
        return pltpu.make_async_remote_copy(
            src_ref=buffer.at[me],
            dst_ref=buffer.at[me],
            send_sem=all_send.at[kind, m],
            recv_sem=all_recv.at[kind, m],
            device_id=peer(m),
            device_id_type=MESH,
        )

    def start(buffer, kind):
        each(lambda m: all_copy(buffer, kind, m).start())

    def arrive(buffer, kind):
        each(lambda m: all_copy(buffer, kind, m).wait_recv())

    rhs = loads.shape[0]
    lower = lax.broadcasted_iota(jnp.int32, (rhs // 2, wide), 1) < half

    def pack(values):
        return jnp.where(lower, values[: rhs // 2], values[rhs // 2 :])

    def unpack(first, second):
        both = jnp.concatenate([first, second], axis=0)
        swapped = pltpu.roll(both, half, 1)
        top = jnp.where(lower, both[: rhs // 2], swapped[rhs // 2 :])
        bottom = jnp.where(lower, swapped[: rhs // 2], both[rhs // 2 :])
        return jnp.concatenate([top, bottom], axis=0)

    def split_matrix(source, high, low):
        step = 128

        def one(i, carry):
            at = pl.ds(pl.multiple_of(i * step, step), step)
            values = source[at, :]
            top = values.astype(BF16)
            high[at, :] = top
            low[at, :] = (values - top.astype(F32)).astype(BF16)
            return carry

        lax.fori_loop(0, source.shape[0] // step, one, 0)

    pl.semaphore_wait(entered, n_row - 1)
    start(idx_all, IDX)
    right_side = face_finish(0, first)
    scaled = weights * right_side
    val_all[0, me] = pack(join(dot(split(scaled), local_hot[...])))
    start(val_all.at[0], RHS)

    def apply(high, low, vectors):
        both = split(vectors)
        return join(dot(both, high[...]) + dot(both, low[...]))

    copies[1].wait()
    values = coarse_in[...]
    top = values.astype(BF16)
    coarse_split[...] = jnp.zeros(coarse_split.shape, BF16)
    coarse_split[:coarse_rows, :] = top
    coarse_split[half : half + coarse_rows, :] = (values - top.astype(F32)).astype(BF16)

    copies[0].wait()
    split_matrix(factor_in, factor_hi, factor_lo)
    local = apply(factor_hi, factor_lo, scaled)
    copies[2].wait()
    split_matrix(schur_in, schur_hi, schur_lo)

    chunk = 256
    chunks = coarse_all // chunk
    small = lax.broadcasted_iota(jnp.int32, (chunk, 2 * wide), 0).astype(F32).astype(BF16)

    def one_column(q, carry):
        for i in range(4):
            @pl.when(q + i > 0)
            def _():
                all_copy(idx_all, IDX, 4 * q + i).wait_recv()
        s = flip(lax.div(me, 4), q, count // 4)
        wanted = jnp.concatenate(
            [jnp.maximum(idx_all[4 * s + i], idx_all[4 * s + i + 1]) for i in (0, 2)], axis=1
        )

        def one_chunk(k, acc):
            start_at = k * chunk
            offset = wanted - start_at
            inside = jnp.logical_and(offset >= 0, offset < chunk)
            offset = jnp.where(inside, offset, -1).astype(F32).astype(BF16)
            picks = jnp.where(small == offset, jnp.ones_like(small), jnp.zeros_like(small))
            return acc + dot(coarse_split[:, pl.ds(start_at, chunk)], picks)

        acc = jnp.zeros((wide, 2 * wide), F32)
        if chunks <= 8:
            for k in range(chunks):
                acc = one_chunk(k, acc)
        else:
            acc = lax.fori_loop(
                0, chunks, lambda k, acc: one_chunk(pl.multiple_of(k, 1), acc), acc
            )
        values = join(acc)
        top = values.astype(BF16)
        at = pl.ds(pl.multiple_of(s * 2 * wide, 2 * wide), 2 * wide)
        columns[:half, at] = top
        columns[half:, at] = (values - top.astype(F32)).astype(BF16)
        return carry

    lax.fori_loop(0, count // 4, one_column, 0)

    for turn in range(2, MOST_SWEEPS + 1):
        inner = scaled - apply(schur_hi, schur_lo, local)
        later = local + apply(factor_hi, factor_lo, inner)
        more = jnp.broadcast_to(elements[...], local.shape) >= turn * ELEM_BASE
        local = jnp.where(more, later, local)
    halved = weights * local
    face_fill(1, halved)
    when_neighbour(can_send, lambda slot: face_copy(1, slot).start())

    def gathered(buffer):
        return split(
            jnp.concatenate([unpack(buffer[s], buffer[s + 1]) for s in range(0, count, 2)], axis=1)
        )

    arrive(val_all.at[0], RHS)
    solved = join(dot_nt(gathered(val_all.at[0]), columns[...]))
    solved = solved + pltpu.roll(solved, half, 1)
    val_all[1, me] = pack(solved)
    start(val_all.at[1], SOL)

    for slot in range(4):
        @pl.when(flags[slot])
        def _():
            near_copy(slot).wait_recv()

        @pl.when(jnp.logical_not(flags[slot]))
        def _():
            near_in[slot] = jnp.full(near_in.shape[1:], -1, jnp.int32)

    def inverse(order_hot):
        order = lax.broadcasted_iota(jnp.int32, (8, face), 1).astype(F32)
        return join(dot_nt(split(order), order_hot[...]))[:1]

    def in_turn(rows):
        joined = None
        for i, row in enumerate(rows):
            wide_place[...] = jnp.full(wide_place.shape, -1, jnp.int32)
            wide_place[:1, :lanes] = row
            row = wide_place[...]
            row = pltpu.roll(row, i * nprim, 1) if i else row
            joined = row if joined is None else jnp.maximum(joined, row)
        return joined[:1]

    west, east, south, north = [near_in[slot] for slot in range(4)]
    target = in_turn(
        [
            numbers,
            look_up(inverse(west_hot), west[1:2] - face, 0),
            east[2:3],
            look_up(inverse(south_hot), south[1:2] - 3 * face, 2 * face),
            north[3:4],
        ]
    )
    wanted_coarse = in_turn([near_out[:1, :]] + [near[:1] for near in (west, east, south, north)])
    place_hot[...] = one_hot(lax.broadcasted_iota(jnp.int32, (unknowns, five), 0), target)

    at = lax.broadcasted_iota(jnp.int32, (wide, five), 0)
    upper = (at >= half).astype(jnp.int32)
    number = upper * coarse_rows + at - upper * half
    number = jnp.where(at - upper * half < coarse_rows, number, -2 * coarse_all)

    def one_pick(s, carry):
        coarse_hot[pl.ds(pl.multiple_of(s * wide, wide), wide), :] = one_hot(
            number, wanted_coarse - s * 2 * coarse_rows
        )
        return carry

    lax.fori_loop(0, count // 2, one_pick, 0)
    halved = face_finish(1, halved)

    def lane_sum(values):
        return jnp.sum(values, axis=1, keepdims=True)

    arrive(val_all.at[1], SOL)
    read = join(dot(gathered(val_all.at[1]), coarse_hot[...]))
    precond = halved + weights * join(dot_nt(split(read), place_hot[...]))
    image = apply(schur_hi, schur_lo, precond)
    rz = lane_sum(scaled * precond)
    pq = lane_sum(precond * image)
    sum_lane = lax.broadcasted_iota(jnp.int32, (rhs, 128), 1)
    sum_case = lax.broadcasted_iota(jnp.int32, (rhs, 128), 0)
    upper_lane, lower_lane = sum_lane == sum_case + rhs, sum_lane == sum_case
    laid = jnp.where(lower_lane, rz, 0.0) + jnp.where(upper_lane, pq, 0.0)
    sum_all[me] = jnp.sum(laid, axis=0, keepdims=True)
    start(sum_all, SUM)
    face_fill(2, image)
    when_neighbour(can_send, lambda slot: face_copy(2, slot).start())
    direction[...] = precond
    loads_out[...] = right_side
    for kind, buffer in enumerate([idx_all, val_all.at[0], val_all.at[1]]):
        each(lambda m: all_copy(buffer, kind, m).wait_send())
    for turn in range(2):
        when_neighbour(can_send, lambda slot: face_copy(turn, slot).wait_send())
    when_neighbour(can_send, lambda slot: near_copy(slot).wait_send())
    image_out[...] = face_finish(2, image)
    arrive(sum_all, SUM)
    sums = sum_all[0]
    for i in range(1, count):
        sums = sums + sum_all[i]
    sums = jnp.broadcast_to(sums, (rhs, 128))
    alpha = lane_sum(jnp.where(lower_lane, sums, 0.0)) / lane_sum(jnp.where(upper_lane, sums, 0.0))
    alpha_out[...] = jnp.broadcast_to(alpha, alpha_out.shape)
    each(lambda m: all_copy(sum_all, SUM, m).wait_send())
    when_neighbour(can_send, lambda slot: face_copy(2, slot).wait_send())


def up(n, to):
    return -(-n // to) * to


def body(
    n_row, n_col, loads, schur, factor, coarse_inverse, elements, west_map, south_map,
    prim_local, prim_coarse,
):
    vectors = loads[0, 0].T
    rhs, unknowns = vectors.shape
    face = unknowns // 4
    coarse_rows, coarse_all = coarse_inverse.shape
    nprim = prim_local.shape[2]
    wide = 2 * up(max(nprim, coarse_rows), 64)
    count = n_row * n_col
    lanes, five = up(nprim, 128), up(5 * nprim, 128)
    vmem = pl.BlockSpec(memory_space=pltpu.VMEM)
    hbm = pl.BlockSpec(memory_space=pl.ANY)
    dma = pltpu.SemaphoreType.DMA
    out = pltpu.VMEM(vectors.shape, F32)
    direction, image, right_side, alpha = pl.pallas_call(
        functools.partial(kernel, n_row, n_col),
        out_shape=(out, out, out, out),
        in_specs=[hbm] * 9,
        out_specs=(vmem, vmem, vmem, vmem),
        scratch_shapes=[
            pltpu.VMEM(vectors.shape, F32),
            pltpu.VMEM((1, 1), jnp.int32),
            pltpu.VMEM((1, face), jnp.int32),
            pltpu.VMEM((1, face), jnp.int32),
            pltpu.VMEM((1, nprim), jnp.int32),
            pltpu.VMEM((1, nprim), jnp.int32),
            pltpu.VMEM((unknowns, unknowns), F32),
            pltpu.VMEM((unknowns, unknowns), F32),
            pltpu.VMEM((coarse_rows, coarse_all), F32),
            pltpu.VMEM((unknowns, unknowns), BF16),
            pltpu.VMEM((unknowns, unknowns), BF16),
            pltpu.VMEM((unknowns, unknowns), BF16),
            pltpu.VMEM((unknowns, unknowns), BF16),
            pltpu.VMEM((wide, coarse_all), BF16),
            pltpu.VMEM((wide, count // 2 * wide), BF16),
            pltpu.VMEM((face, face), BF16),
            pltpu.VMEM((face, face), BF16),
            pltpu.VMEM((unknowns, wide), BF16),
            pltpu.VMEM((count // 2 * wide, five), BF16),
            pltpu.VMEM((unknowns, five), BF16),
            pltpu.VMEM((8, wide), jnp.int32),
            pltpu.VMEM((8, five), jnp.int32),
            pltpu.VMEM((count, 1, wide), jnp.int32),
            pltpu.VMEM((2, count, rhs // 2, wide), F32),
            pltpu.VMEM((count, 1, 128), F32),
            pltpu.VMEM((3, 4, rhs, face), F32),
            pltpu.VMEM((3, 4, rhs, face), F32),
            pltpu.VMEM((4, lanes), jnp.int32),
            pltpu.VMEM((4, 4, lanes), jnp.int32),
            dma((9,)),
            dma((3, 4)),
            dma((3, 4)),
            dma((4,)),
            dma((4,)),
            dma((4, count)),
            dma((4, count)),
            pltpu.SemaphoreType.REGULAR,
        ],
        compiler_params=pltpu.CompilerParams(collective_id=0, has_side_effects=True),
    )(
        vectors, schur[0, 0], factor[0, 0], coarse_inverse, elements,
        west_map[0], south_map[0], prim_local[0], prim_coarse[0],
    )
    solution = alpha * direction
    residual = right_side - alpha * image
    return solution.T[None, None], residual.T[None, None]


def solution(mesh):
    placed = (
        P("row", "col", None, None),
        P("row", "col", None, None),
        P("row", "col", None, None),
        P(("row", "col"), None),
        P("row", "col"),
        P("row", "col", None),
        P("row", "col", None),
        P("row", "col", None),
        P("row", "col", None),
    )
    return jax.shard_map(
        functools.partial(body, mesh.shape["row"], mesh.shape["col"]),
        mesh=mesh,
        in_specs=placed,
        out_specs=(P("row", "col", None, None), P("row", "col", None, None)),
        check_vma=False,
    )
```

```python
import functools

import jax
import jax.numpy as jnp
from jax import lax
from jax.experimental import pallas as pl
from jax.experimental.pallas import tpu as pltpu
from jax.sharding import PartitionSpec as P

ELEM_BASE = 4096
MOST_SWEEPS = 3
MESH = pl.DeviceIdType.MESH
F32, BF16 = jnp.float32, jnp.bfloat16
NT = (((1,), (1,)), ((), ()))
IDX, RHS, SOL, SUM = range(4)


def split(values):
    high = values.astype(BF16).astype(F32)
    return jnp.concatenate([high, values - high], axis=0).astype(BF16)


def join(stacked):
    rows = stacked.shape[0] // 2
    return stacked[:rows] + stacked[rows:]


def one_hot(numbers, wanted):
    return jnp.where(numbers == wanted, 1.0, 0.0).astype(BF16)


def dot(a, b):
    return jnp.dot(a, b, preferred_element_type=F32)


def dot_nt(a, b):
    return lax.dot_general(a, b, NT, preferred_element_type=F32)


def flip(value, mask, size):
    out, weight = 0, 1
    while weight < size:
        bit = lax.rem(lax.div(value, weight), 2)
        if isinstance(mask, int):
            bit = 1 - bit if (mask // weight) % 2 else bit
        else:
            bit = lax.rem(bit + lax.rem(lax.div(mask, weight), 2), 2)
        out, weight = out + weight * bit, 2 * weight
    return out


def kernel(
    n_row, n_col, loads_hbm, schur_hbm, factor_hbm, coarse_hbm, elements_hbm, west_hbm, south_hbm,
    local_hbm, prim_hbm, direction, image_out, loads_out, alpha_out,
    loads, elements, west_map, south_map, prim_local, prim_coarse,
    schur_in, factor_in, coarse_in, schur_hi, schur_lo, factor_hi, factor_lo,
    coarse_split, columns, west_hot, south_hot, local_hot, coarse_hot, place_hot,
    place, wide_place, idx_all, val_all, sum_all, face_out, face_in, near_out, near_in,
    copy_sem, face_send, face_recv, near_send, near_recv, all_send, all_recv, entered,
):
    a, c = lax.axis_index("row"), lax.axis_index("col")
    unknowns = loads.shape[1]
    face = unknowns // 4
    wide = local_hot.shape[1]
    half = wide // 2
    count = n_row * n_col
    me = a * n_col + c
    odd = lax.rem(me, 2)
    coarse_rows, coarse_all = coarse_in.shape
    nprim = prim_local.shape[1]
    lanes = near_out.shape[1]
    five = place_hot.shape[0]

    copies = [
        pltpu.make_async_copy(src, dst, copy_sem.at[i])
        for i, (src, dst) in enumerate(
            [
                (factor_hbm, factor_in), (coarse_hbm, coarse_in), (schur_hbm, schur_in),
                (loads_hbm, loads), (west_hbm, west_map), (south_hbm, south_map),
                (local_hbm, prim_local), (prim_hbm, prim_coarse), (elements_hbm, elements),
            ]
        )
    ]
    barrier = pltpu.get_barrier_semaphore()
    column_mates = [(flip(a, m, n_row), c) for m in range(1, n_row)]
    row_mates = [(a, flip(c, m, n_col)) for m in range(1, n_col)]
    for mate in row_mates + column_mates:
        pl.semaphore_signal(barrier, inc=1, device_id=mate, device_id_type=MESH)
    for copy in copies[3:] + copies[:3]:
        copy.start()

    rows_of = [flip(a, m, n_row) for m in range(n_row)]
    cols_of = [flip(c, m, n_col) for m in range(n_col)]

    def peer(m):
        if not isinstance(m, int):
            return (flip(a, lax.div(m, n_col), n_row), flip(c, lax.rem(m, n_col), n_col))
        return (rows_of[m // n_col], cols_of[m % n_col])

    def each(work):
        if count <= 64:
            for m in range(count - 1, 0, -1):
                work(m)
        else:
            lax.fori_loop(1, count, lambda d, carry: (work(count - d), carry)[1], 0)

    for copy in copies[3:]:
        copy.wait()

    def hot(order_ref):
        return one_hot(lax.broadcasted_iota(jnp.int32, (face, face), 0), order_ref[...])

    west_hot[...] = hot(west_map)
    south_hot[...] = hot(south_map)

    lane = lax.broadcasted_iota(jnp.int32, (1, unknowns), 1)
    flags = [c > 0, c < n_col - 1, a > 0, a < n_row - 1]
    halves = [jnp.where(flag, 0.5, 1.0).astype(F32) for flag in flags]
    weights = jnp.where(
        lane < face,
        halves[0],
        jnp.where(lane < 2 * face, halves[1], jnp.where(lane < 3 * face, halves[2], halves[3])),
    )
    targets = [(a, c + 1), (a, c - 1), (a + 1, c), (a - 1, c)]
    can_send = [flags[1], flags[0], flags[3], flags[2]]

    def face_copy(turn, slot):
        return pltpu.make_async_remote_copy(
            src_ref=face_out.at[turn, slot],
            dst_ref=face_in.at[turn, slot],
            send_sem=face_send.at[turn, slot],
            recv_sem=face_recv.at[turn, slot],
            device_id=targets[slot],
            device_id_type=MESH,
        )

    def near_copy(slot):
        return pltpu.make_async_remote_copy(
            src_ref=near_out,
            dst_ref=near_in.at[slot],
            send_sem=near_send.at[slot],
            recv_sem=near_recv.at[slot],
            device_id=targets[slot],
            device_id_type=MESH,
        )

    def face_fill(turn, values):
        face_out[turn, 0] = values[:, face : 2 * face]
        face_out[turn, 2] = values[:, 3 * face :]
        face_out[turn, 1] = join(dot_nt(split(values[:, :face]), west_hot[...]))
        face_out[turn, 3] = join(dot_nt(split(values[:, 2 * face : 3 * face]), south_hot[...]))

    def when_neighbour(present, work):
        for slot in range(4):
            @pl.when(present[slot])
            def _():
                work(slot)

    def face_finish(turn, values):
        for slot in range(4):
            @pl.when(flags[slot])
            def _():
                face_copy(turn, slot).wait_recv()

            @pl.when(jnp.logical_not(flags[slot]))
            def _():
                face_in[turn, slot] = jnp.zeros(face_in.shape[2:], F32)
        adds = [
            join(dot(split(face_in[turn, 0]), west_hot[...])),
            face_in[turn, 1],
            join(dot(split(face_in[turn, 2]), south_hot[...])),
            face_in[turn, 3],
        ]
        return values + jnp.concatenate(adds, axis=1)

    first = loads[...]
    face_fill(0, first)
    pl.semaphore_wait(barrier, n_row + n_col - 2)
    when_neighbour(can_send, lambda slot: face_copy(0, slot).start())
    for mate in column_mates:
        pl.semaphore_signal(entered, inc=1, device_id=mate, device_id_type=MESH)

    def placed(source):
        place[...] = jnp.full(place.shape, -1, jnp.int32)
        place[:1, :nprim] = source[...]
        base = place[...]
        return base, pltpu.roll(base, half, 1)

    base, rolled = placed(prim_coarse)
    own_coarse = jnp.where(odd == 1, rolled, base)[:1]
    idx_all[me] = own_coarse
    near_out[...] = jnp.full(near_out.shape, -1, jnp.int32)
    near_out[:1, :nprim] = prim_coarse[...]
    near_out[1:2, :nprim] = prim_local[...]
    numbers = near_out[1:2, :]
    depth = lax.broadcasted_iota(jnp.int32, (face, lanes), 0)

    def look_up(table, numbers, offset):
        inside = jnp.logical_and(numbers >= 0, numbers < face)
        table = jnp.broadcast_to(table, (8, face)).astype(F32)
        found = join(dot(split(table), one_hot(depth, numbers)))[:1]
        return jnp.where(inside, found.astype(jnp.int32) + offset, -1)

    near_out[2:3, :] = look_up(west_map[...], numbers, face)
    near_out[3:4, :] = look_up(south_map[...], numbers - 2 * face, 3 * face)
    when_neighbour(can_send, lambda slot: near_copy(slot).start())

    own_local = jnp.maximum(*placed(prim_local))[:1]
    rows_iota = lax.broadcasted_iota(jnp.int32, (unknowns, wide), 0)
    local_hot[...] = one_hot(rows_iota, own_local)

    def all_copy(buffer, kind, m):
        return pltpu.make_async_remote_copy(
            src_ref=buffer.at[me],
            dst_ref=buffer.at[me],
            send_sem=all_send.at[kind, m],
            recv_sem=all_recv.at[kind, m],
            device_id=peer(m),
            device_id_type=MESH,
        )

    def start(buffer, kind):
        each(lambda m: all_copy(buffer, kind, m).start())

    def arrive(buffer, kind):
        each(lambda m: all_copy(buffer, kind, m).wait_recv())

    rhs = loads.shape[0]
    lower = lax.broadcasted_iota(jnp.int32, (rhs // 2, wide), 1) < half

    def pack(values):
        return jnp.where(lower, values[: rhs // 2], values[rhs // 2 :])

    square = (rhs, wide)
    stays = (lax.broadcasted_iota(jnp.int32, square, 1) < half) == (
        lax.broadcasted_iota(jnp.int32, square, 0) < rhs // 2
    )

    def unpack(first, second):
        both = jnp.concatenate([first, second], axis=0)
        return jnp.where(stays, both, pltpu.roll(pltpu.roll(both, half, 1), rhs // 2, 0))

    def split_matrix(source, high, low):
        step = 128

        def one(i, carry):
            at = pl.ds(pl.multiple_of(i * step, step), step)
            values = source[at, :]
            top = values.astype(BF16)
            high[at, :] = top
            low[at, :] = (values - top.astype(F32)).astype(BF16)
            return carry

        lax.fori_loop(0, source.shape[0] // step, one, 0)

    chunk = coarse_split.shape[1]
    chunks = coarse_all // chunk
    part = coarse_split.shape[0] // chunks // 2

    def over_chunks(work, carry):
        if chunks <= 8:
            for k in range(chunks):
                carry = work(k, carry)
            return carry
        return lax.fori_loop(0, chunks, work, carry)

    def split_coarse():
        copies[1].wait()
        columns[...] = jnp.zeros(columns.shape, BF16)
        if coarse_rows < part:
            coarse_split[...] = jnp.zeros(coarse_split.shape, BF16)

        def one(k, carry):
            at = k * chunk if isinstance(k, int) else pl.multiple_of(k * chunk, chunk)
            rows = 2 * part * k if isinstance(k, int) else pl.multiple_of(2 * part * k, 2 * part)
            values = coarse_in[:, pl.ds(at, chunk)]
            top = values.astype(BF16)
            coarse_split[pl.ds(rows, coarse_rows), :] = top
            coarse_split[pl.ds(rows + part, coarse_rows), :] = (values - top.astype(F32)).astype(BF16)
            return carry

        over_chunks(one, 0)

    early = c < n_col // 2

    def announce():
        pl.semaphore_wait(entered, n_row - 1)
        start(idx_all, IDX)

    def split_schur():
        copies[2].wait()
        split_matrix(schur_in, schur_hi, schur_lo)

    copies[0].wait()
    split_matrix(factor_in, factor_hi, factor_lo)
    split_coarse()
    pl.when(early)(split_schur)
    pl.when(jnp.logical_not(early))(announce)
    right_side = face_finish(0, first)
    scaled = weights * right_side
    val_all[0, me] = pack(join(dot(split(scaled), local_hot[...])))
    pl.when(early)(announce)
    start(val_all.at[0], RHS)

    def apply(high, low, vectors):
        both = split(vectors)
        return join(dot(both, high[...]) + dot(both, low[...]))

    pl.when(jnp.logical_not(early))(split_schur)
    local = apply(factor_hi, factor_lo, scaled)
    for turn in range(2, MOST_SWEEPS):
        inner = scaled - apply(schur_hi, schur_lo, local)
        later = local + apply(factor_hi, factor_lo, inner)
        more = jnp.broadcast_to(elements[...], local.shape) >= turn * ELEM_BASE
        local = jnp.where(more, later, local)
    small = lax.broadcasted_iota(jnp.int32, (chunk, 2 * wide), 0).astype(F32).astype(BF16)

    blocks = n_col // 4

    def one_column(step, carry):
        q = lax.rem(step, n_row) * blocks + lax.div(step, n_row)
        for i in range(4):
            @pl.when(q + i > 0)
            def _():
                all_copy(idx_all, IDX, 4 * q + i).wait_recv()
        s = flip(lax.div(me, 4), q, count // 4)
        wanted = jnp.concatenate(
            [jnp.maximum(idx_all[4 * s + i], idx_all[4 * s + i + 1]) for i in (0, 2)], axis=1
        )

        which = jnp.right_shift(wanted, chunk.bit_length() - 1)
        offset = jnp.bitwise_and(wanted, chunk - 1).astype(F32).astype(BF16)
        picks = jnp.where(small == offset, jnp.ones_like(small), jnp.zeros_like(small))

        if chunks <= 8:
            taken = dot(coarse_split[...], picks)
            acc = jnp.zeros((2 * part, 2 * wide), F32)
            for k in range(chunks):
                acc = jnp.where(which == k, taken[2 * part * k : 2 * part * (k + 1)], acc)
        else:

            def one_chunk(k, acc):
                rows = pl.ds(pl.multiple_of(2 * part * k, 2 * part), 2 * part)
                return jnp.where(which == k, dot(coarse_split[rows, :], picks), acc)

            acc = lax.fori_loop(0, chunks, one_chunk, jnp.zeros((2 * part, 2 * wide), F32))
        values = join(acc)
        top = values.astype(BF16)
        at = pl.ds(pl.multiple_of(s * 2 * wide, 2 * wide), 2 * wide)
        columns[:part, at] = top
        columns[half : half + part, at] = (values - top.astype(F32)).astype(BF16)
        return carry

    lax.fori_loop(0, count // 4, one_column, 0)

    def gathered(buffer):
        return split(
            jnp.concatenate([unpack(buffer[s], buffer[s + 1]) for s in range(0, count, 2)], axis=1)
        )

    arrive(val_all.at[0], RHS)
    solved = join(dot_nt(gathered(val_all.at[0]), columns[...]))
    solved = solved + pltpu.roll(solved, half, 1)
    val_all[1, me] = pack(solved)
    start(val_all.at[1], SOL)

    for turn in range(MOST_SWEEPS, MOST_SWEEPS + 1):
        inner = scaled - apply(schur_hi, schur_lo, local)
        later = local + apply(factor_hi, factor_lo, inner)
        more = jnp.broadcast_to(elements[...], local.shape) >= turn * ELEM_BASE
        local = jnp.where(more, later, local)
    halved = weights * local
    face_fill(1, halved)
    when_neighbour(can_send, lambda slot: face_copy(1, slot).start())

    for slot in range(4):
        @pl.when(flags[slot])
        def _():
            near_copy(slot).wait_recv()

        @pl.when(jnp.logical_not(flags[slot]))
        def _():
            near_in[slot] = jnp.full(near_in.shape[1:], -1, jnp.int32)

    def inverse(order_hot):
        order = lax.broadcasted_iota(jnp.int32, (8, face), 1).astype(F32)
        return join(dot_nt(split(order), order_hot[...]))[:1]

    def in_turn(rows):
        joined = None
        for i, row in enumerate(rows):
            wide_place[...] = jnp.full(wide_place.shape, -1, jnp.int32)
            wide_place[:1, :lanes] = row
            row = wide_place[...]
            row = pltpu.roll(row, i * nprim, 1) if i else row
            joined = row if joined is None else jnp.maximum(joined, row)
        return joined[:1]

    west, east, south, north = [near_in[slot] for slot in range(4)]
    target = in_turn(
        [
            numbers,
            look_up(inverse(west_hot), west[1:2] - face, 0),
            east[2:3],
            look_up(inverse(south_hot), south[1:2] - 3 * face, 2 * face),
            north[3:4],
        ]
    )
    wanted_coarse = in_turn([near_out[:1, :]] + [near[:1] for near in (west, east, south, north)])
    target = jnp.broadcast_to(target.astype(F32), (8, five)).T[:, :1].astype(jnp.int32)
    place_hot[...] = one_hot(lax.broadcasted_iota(jnp.int32, (five, unknowns), 1), target)

    at = lax.broadcasted_iota(jnp.int32, (wide, five), 0)
    upper = (at >= half).astype(jnp.int32)
    number = upper * coarse_rows + at - upper * half
    number = jnp.where(at - upper * half < coarse_rows, number, -2 * coarse_all)

    def one_pick(s, carry):
        coarse_hot[pl.ds(pl.multiple_of(s * wide, wide), wide), :] = one_hot(
            number, wanted_coarse - s * 2 * coarse_rows
        )
        return carry

    lax.fori_loop(0, count // 2, one_pick, 0)
    halved = face_finish(1, halved)

    def lane_sum(values):
        return jnp.sum(values, axis=1, keepdims=True)

    arrive(val_all.at[1], SOL)
    read = join(dot(gathered(val_all.at[1]), coarse_hot[...]))
    precond = halved + weights * join(dot(split(read), place_hot[...]))
    image = apply(schur_hi, schur_lo, precond)
    rz = lane_sum(scaled * precond)
    pq = lane_sum(precond * image)
    sum_lane = lax.broadcasted_iota(jnp.int32, (rhs, 128), 1)
    sum_case = lax.broadcasted_iota(jnp.int32, (rhs, 128), 0)
    upper_lane, lower_lane = sum_lane == sum_case + rhs, sum_lane == sum_case
    laid = jnp.where(lower_lane, rz, 0.0) + jnp.where(upper_lane, pq, 0.0)
    sum_all[me] = jnp.sum(laid, axis=0, keepdims=True)
    start(sum_all, SUM)
    face_fill(2, image)
    when_neighbour(can_send, lambda slot: face_copy(2, slot).start())
    direction[...] = precond
    loads_out[...] = right_side
    for kind, buffer in enumerate([idx_all, val_all.at[0], val_all.at[1]]):
        each(lambda m: all_copy(buffer, kind, m).wait_send())
    for turn in range(2):
        when_neighbour(can_send, lambda slot: face_copy(turn, slot).wait_send())
    when_neighbour(can_send, lambda slot: near_copy(slot).wait_send())
    image_out[...] = face_finish(2, image)
    arrive(sum_all, SUM)
    parts = [sum_all[i] for i in range(count)]
    while len(parts) > 1:
        parts = [x + y for x, y in zip(parts[::2], parts[1::2])]
    sums = jnp.broadcast_to(parts[0], (rhs, 128))
    alpha = lane_sum(jnp.where(lower_lane, sums, 0.0)) / lane_sum(jnp.where(upper_lane, sums, 0.0))
    alpha_out[...] = jnp.broadcast_to(alpha, alpha_out.shape)
    each(lambda m: all_copy(sum_all, SUM, m).wait_send())
    when_neighbour(can_send, lambda slot: face_copy(2, slot).wait_send())


def up(n, to):
    return -(-n // to) * to


def body(
    n_row, n_col, loads, schur, factor, coarse_inverse, elements, west_map, south_map,
    prim_local, prim_coarse,
):
    vectors = loads[0, 0].T
    rhs, unknowns = vectors.shape
    face = unknowns // 4
    coarse_rows, coarse_all = coarse_inverse.shape
    nprim = prim_local.shape[2]
    wide = 2 * up(max(nprim, coarse_rows), 64)
    count = n_row * n_col
    lanes, five = up(nprim, 128), up(5 * nprim, 128)
    vmem = pl.BlockSpec(memory_space=pltpu.VMEM)
    hbm = pl.BlockSpec(memory_space=pl.ANY)
    dma = pltpu.SemaphoreType.DMA
    out = pltpu.VMEM(vectors.shape, F32)
    direction, image, right_side, alpha = pl.pallas_call(
        functools.partial(kernel, n_row, n_col),
        out_shape=(out, out, out, out),
        in_specs=[hbm] * 9,
        out_specs=(vmem, vmem, vmem, vmem),
        scratch_shapes=[
            pltpu.VMEM(vectors.shape, F32),
            pltpu.VMEM((1, 1), jnp.int32),
            pltpu.VMEM((1, face), jnp.int32),
            pltpu.VMEM((1, face), jnp.int32),
            pltpu.VMEM((1, nprim), jnp.int32),
            pltpu.VMEM((1, nprim), jnp.int32),
            pltpu.VMEM((unknowns, unknowns), F32),
            pltpu.VMEM((unknowns, unknowns), F32),
            pltpu.VMEM((coarse_rows, coarse_all), F32),
            pltpu.VMEM((unknowns, unknowns), BF16),
            pltpu.VMEM((unknowns, unknowns), BF16),
            pltpu.VMEM((unknowns, unknowns), BF16),
            pltpu.VMEM((unknowns, unknowns), BF16),
            pltpu.VMEM((coarse_all // face * 2 * up(coarse_rows, 16), face), BF16),
            pltpu.VMEM((wide, count // 2 * wide), BF16),
            pltpu.VMEM((face, face), BF16),
            pltpu.VMEM((face, face), BF16),
            pltpu.VMEM((unknowns, wide), BF16),
            pltpu.VMEM((count // 2 * wide, five), BF16),
            pltpu.VMEM((five, unknowns), BF16),
            pltpu.VMEM((8, wide), jnp.int32),
            pltpu.VMEM((8, five), jnp.int32),
            pltpu.VMEM((count, 1, wide), jnp.int32),
            pltpu.VMEM((2, count, rhs // 2, wide), F32),
            pltpu.VMEM((count, 1, 128), F32),
            pltpu.VMEM((3, 4, rhs, face), F32),
            pltpu.VMEM((3, 4, rhs, face), F32),
            pltpu.VMEM((4, lanes), jnp.int32),
            pltpu.VMEM((4, 4, lanes), jnp.int32),
            dma((9,)),
            dma((3, 4)),
            dma((3, 4)),
            dma((4,)),
            dma((4,)),
            dma((4, count)),
            dma((4, count)),
            pltpu.SemaphoreType.REGULAR,
        ],
        compiler_params=pltpu.CompilerParams(collective_id=0, has_side_effects=True),
    )(
        vectors, schur[0, 0], factor[0, 0], coarse_inverse, elements,
        west_map[0], south_map[0], prim_local[0], prim_coarse[0],
    )
    solution = alpha * direction
    residual = right_side - alpha * image
    return solution.T[None, None], residual.T[None, None]


def solution(mesh):
    placed = (
        P("row", "col", None, None),
        P("row", "col", None, None),
        P("row", "col", None, None),
        P(("row", "col"), None),
        P("row", "col"),
        P("row", "col", None),
        P("row", "col", None),
        P("row", "col", None),
        P("row", "col", None),
    )
    return jax.shard_map(
        functools.partial(body, mesh.shape["row"], mesh.shape["col"]),
        mesh=mesh,
        in_specs=placed,
        out_specs=(P("row", "col", None, None), P("row", "col", None, None)),
        check_vma=False,
    )
```

```python
import functools

import jax
import jax.numpy as jnp
from jax import lax
from jax.experimental import pallas as pl
from jax.experimental.pallas import tpu as pltpu
from jax.sharding import PartitionSpec as P

ELEM_BASE = 4096
MOST_SWEEPS = 3
MESH = pl.DeviceIdType.MESH
F32, BF16 = jnp.float32, jnp.bfloat16
NT = (((1,), (1,)), ((), ()))
RHS, SOL, SUM = range(3)


def split(values):
    high = values.astype(BF16).astype(F32)
    return jnp.concatenate([high, values - high], axis=0).astype(BF16)


def join(stacked):
    rows = stacked.shape[0] // 2
    return stacked[:rows] + stacked[rows:]


def one_hot(numbers, wanted):
    return jnp.where(numbers == wanted, 1.0, 0.0).astype(BF16)


def dot(a, b):
    return jnp.dot(a, b, preferred_element_type=F32)


def dot_nt(a, b):
    return lax.dot_general(a, b, NT, preferred_element_type=F32)


def flip(value, mask, size):
    out, weight = 0, 1
    while weight < size:
        bit = lax.rem(lax.div(value, weight), 2)
        if isinstance(mask, int):
            bit = 1 - bit if (mask // weight) % 2 else bit
        else:
            bit = lax.rem(bit + lax.rem(lax.div(mask, weight), 2), 2)
        out, weight = out + weight * bit, 2 * weight
    return out


def kernel(
    n_row, n_col, loads_hbm, schur_hbm, factor_hbm, coarse_hbm, elements_hbm, west_hbm, south_hbm,
    local_hbm, prim_hbm, direction, image_out, loads_out, alpha_out,
    loads, elements, west_map, south_map, prim_local, prim_coarse,
    schur_in, factor_in, coarse_in, schur_hi, schur_lo, factor_hi, factor_lo,
    coarse_split, columns, west_hot, south_hot, local_hot, coarse_hot, place_hot, spread_hi, spread_lo, local,
    place, wide_place, idx_all, val_all, sum_all, face_out, face_in, near_out, near_in,
    copy_sem, face_send, face_recv, near_send, near_recv, idx_send, idx_recv, all_send, all_recv, entered,
):
    a, c = lax.axis_index("row"), lax.axis_index("col")
    unknowns = loads.shape[1]
    face = unknowns // 4
    wide = local_hot.shape[1]
    half = wide // 2
    count = n_row * n_col
    me = a * n_col + c
    odd = lax.rem(me, 2)
    coarse_rows, coarse_all = coarse_in.shape
    nprim = prim_local.shape[1]
    lanes = near_out.shape[1]
    five = place_hot.shape[0]

    copies = [
        pltpu.make_async_copy(src, dst, copy_sem.at[i])
        for i, (src, dst) in enumerate(
            [
                (factor_hbm, factor_in), (coarse_hbm, coarse_in), (schur_hbm, schur_in),
                (loads_hbm, loads), (west_hbm, west_map), (south_hbm, south_map),
                (local_hbm, prim_local), (prim_hbm, prim_coarse), (elements_hbm, elements),
            ]
        )
    ]
    barrier = pltpu.get_barrier_semaphore()
    column_mates = [(flip(a, m, n_row), c) for m in range(1, n_row)]
    row_mates = [(a, flip(c, m, n_col)) for m in range(1, n_col)]
    for mate in row_mates + column_mates:
        pl.semaphore_signal(barrier, inc=1, device_id=mate, device_id_type=MESH)
    for copy in copies[3:] + copies[:3]:
        copy.start()

    rows_of = [flip(a, m, n_row) for m in range(n_row)]
    cols_of = [flip(c, m, n_col) for m in range(n_col)]

    def peer(m):
        if not isinstance(m, int):
            return (flip(a, lax.div(m, n_col), n_row), flip(c, lax.rem(m, n_col), n_col))
        return (rows_of[m // n_col], cols_of[m % n_col])

    def each(work):
        if count <= 64:
            for m in range(count - 1, 0, -1):
                work(m)
        else:
            lax.fori_loop(1, count, lambda d, carry: (work(count - d), carry)[1], 0)

    for copy in copies[3:]:
        copy.wait()

    def hot(order_ref):
        return one_hot(lax.broadcasted_iota(jnp.int32, (face, face), 0), order_ref[...])

    west_hot[...] = hot(west_map)
    south_hot[...] = hot(south_map)

    lane = lax.broadcasted_iota(jnp.int32, (1, unknowns), 1)
    flags = [c > 0, c < n_col - 1, a > 0, a < n_row - 1]
    halves = [jnp.where(flag, 0.5, 1.0).astype(F32) for flag in flags]
    weights = jnp.where(
        lane < face,
        halves[0],
        jnp.where(lane < 2 * face, halves[1], jnp.where(lane < 3 * face, halves[2], halves[3])),
    )
    targets = [(a, c + 1), (a, c - 1), (a + 1, c), (a - 1, c)]
    can_send = [flags[1], flags[0], flags[3], flags[2]]

    def face_copy(turn, slot):
        return pltpu.make_async_remote_copy(
            src_ref=face_out.at[turn, slot],
            dst_ref=face_in.at[turn, slot],
            send_sem=face_send.at[turn, slot],
            recv_sem=face_recv.at[turn, slot],
            device_id=targets[slot],
            device_id_type=MESH,
        )

    def near_copy(slot):
        return pltpu.make_async_remote_copy(
            src_ref=near_out,
            dst_ref=near_in.at[slot],
            send_sem=near_send.at[slot],
            recv_sem=near_recv.at[slot],
            device_id=targets[slot],
            device_id_type=MESH,
        )

    def face_fill(turn, values):
        face_out[turn, 0] = values[:, face : 2 * face]
        face_out[turn, 2] = values[:, 3 * face :]
        face_out[turn, 1] = join(dot_nt(split(values[:, :face]), west_hot[...]))
        face_out[turn, 3] = join(dot_nt(split(values[:, 2 * face : 3 * face]), south_hot[...]))

    def when_neighbour(present, work):
        for slot in range(4):
            @pl.when(present[slot])
            def _():
                work(slot)

    def face_finish(turn, values):
        for slot in range(4):
            @pl.when(flags[slot])
            def _():
                face_copy(turn, slot).wait_recv()

            @pl.when(jnp.logical_not(flags[slot]))
            def _():
                face_in[turn, slot] = jnp.zeros(face_in.shape[2:], F32)
        adds = [
            join(dot(split(face_in[turn, 0]), west_hot[...])),
            face_in[turn, 1],
            join(dot(split(face_in[turn, 2]), south_hot[...])),
            face_in[turn, 3],
        ]
        return values + jnp.concatenate(adds, axis=1)

    first = loads[...]
    face_fill(0, first)
    pl.semaphore_wait(barrier, n_row + n_col - 2)
    when_neighbour(can_send, lambda slot: face_copy(0, slot).start())
    for mate in column_mates:
        pl.semaphore_signal(entered, inc=1, device_id=mate, device_id_type=MESH)

    def placed(source):
        place[...] = jnp.full(place.shape, -1, jnp.int32)
        place[:1, :nprim] = source[...]
        base = place[...]
        return base, pltpu.roll(base, half, 1)

    base, rolled = placed(prim_coarse)
    own_coarse = jnp.where(odd == 1, rolled, base)[:1]
    idx_all[me] = own_coarse
    near_out[...] = jnp.full(near_out.shape, -1, jnp.int32)
    near_out[:1, :nprim] = prim_coarse[...]
    near_out[1:2, :nprim] = prim_local[...]
    numbers = near_out[1:2, :]
    depth = lax.broadcasted_iota(jnp.int32, (face, lanes), 0)

    def look_up(table, numbers, offset):
        inside = jnp.logical_and(numbers >= 0, numbers < face)
        table = jnp.broadcast_to(table, (8, face)).astype(F32)
        found = join(dot(split(table), one_hot(depth, numbers)))[:1]
        return jnp.where(inside, found.astype(jnp.int32) + offset, -1)

    near_out[2:3, :] = look_up(west_map[...], numbers, face)
    near_out[3:4, :] = look_up(south_map[...], numbers - 2 * face, 3 * face)
    when_neighbour(can_send, lambda slot: near_copy(slot).start())

    own_local = jnp.maximum(*placed(prim_local))[:1]
    rows_iota = lax.broadcasted_iota(jnp.int32, (unknowns, wide), 0)
    local_hot[...] = one_hot(rows_iota, own_local)

    def idx_copy(m):
        return pltpu.make_async_remote_copy(
            src_ref=idx_all.at[me],
            dst_ref=idx_all.at[me],
            send_sem=idx_send,
            recv_sem=idx_recv.at[m // 4 if isinstance(m, int) else lax.div(m, 4)],
            device_id=peer(m),
            device_id_type=MESH,
        )

    def all_copy(buffer, kind, m):
        return pltpu.make_async_remote_copy(
            src_ref=buffer.at[me],
            dst_ref=buffer.at[me],
            send_sem=all_send.at[kind],
            recv_sem=all_recv.at[kind],
            device_id=peer(m),
            device_id_type=MESH,
        )

    def start(buffer, kind):
        each(lambda m: all_copy(buffer, kind, m).start())

    def await_some(buffer, sent, semaphore):
        slots = buffer.at[pl.ds(0, sent)]
        pltpu.make_async_copy(slots, slots, semaphore).wait()

    def await_all(buffer, semaphore):
        await_some(buffer, count - 1, semaphore)

    def arrive(buffer, kind):
        await_all(buffer, all_recv.at[kind])

    rhs = loads.shape[0]
    lower = lax.broadcasted_iota(jnp.int32, (rhs // 2, wide), 1) < half

    def pack(values):
        return jnp.where(lower, values[: rhs // 2], values[rhs // 2 :])

    square = (rhs, wide)
    stays = (lax.broadcasted_iota(jnp.int32, square, 1) < half) == (
        lax.broadcasted_iota(jnp.int32, square, 0) < rhs // 2
    )

    def unpack(first, second):
        both = jnp.concatenate([first, second], axis=0)
        return jnp.where(stays, both, pltpu.roll(pltpu.roll(both, half, 1), rhs // 2, 0))

    def split_matrix(source, high, low):
        step = 128

        def one(i, carry):
            at = pl.ds(pl.multiple_of(i * step, step), step)
            values = source[at, :]
            top = values.astype(BF16)
            high[at, :] = top
            low[at, :] = (values - top.astype(F32)).astype(BF16)
            return carry

        lax.fori_loop(0, source.shape[0] // step, one, 0)

    chunk = coarse_split.shape[1]
    chunks = coarse_all // chunk
    part = coarse_split.shape[0] // chunks // 2

    def over_chunks(work, carry):
        if chunks <= 8:
            for k in range(chunks):
                carry = work(k, carry)
            return carry
        return lax.fori_loop(0, chunks, work, carry)

    def split_coarse():
        copies[1].wait()
        columns[...] = jnp.zeros(columns.shape, BF16)
        if coarse_rows < part:
            coarse_split[...] = jnp.zeros(coarse_split.shape, BF16)

        def one(k, carry):
            at = k * chunk if isinstance(k, int) else pl.multiple_of(k * chunk, chunk)
            rows = 2 * part * k if isinstance(k, int) else pl.multiple_of(2 * part * k, 2 * part)
            values = coarse_in[:, pl.ds(at, chunk)]
            top = values.astype(BF16)
            coarse_split[pl.ds(rows, coarse_rows), :] = top
            coarse_split[pl.ds(rows + part, coarse_rows), :] = (values - top.astype(F32)).astype(BF16)
            return carry

        over_chunks(one, 0)

    early = c < n_col // 2

    def announce():
        pl.semaphore_wait(entered, n_row - 1)
        each(lambda m: idx_copy(m).start())

    def split_schur():
        copies[2].wait()
        split_matrix(schur_in, schur_hi, schur_lo)

    copies[0].wait()
    split_matrix(factor_in, factor_hi, factor_lo)
    split_coarse()
    pl.when(early)(split_schur)
    pl.when(jnp.logical_not(early))(announce)
    right_side = face_finish(0, first)
    scaled = weights * right_side
    val_all[0, me] = pack(join(dot(split(scaled), local_hot[...])))
    pl.when(early)(announce)
    start(val_all.at[0], RHS)

    def apply(high, low, vectors):
        both = split(vectors)
        return join(dot(both, high[...]) + dot(both, low[...]))

    pl.when(jnp.logical_not(early))(split_schur)
    local[...] = apply(factor_hi, factor_lo, scaled)

    def sweep(turn):
        now = local[...]
        inner = scaled - apply(schur_hi, schur_lo, now)
        later = now + apply(factor_hi, factor_lo, inner)
        more = jnp.broadcast_to(elements[...], now.shape) >= turn * ELEM_BASE
        local[...] = jnp.where(more, later, now)

    def last_sweep():
        sweep(MOST_SWEEPS)
        face_fill(1, weights * local[...])
        when_neighbour(can_send, lambda slot: face_copy(1, slot).start())

    for turn in range(2, MOST_SWEEPS):
        sweep(turn)
    pl.when(jnp.logical_not(early))(last_sweep)
    small = lax.broadcasted_iota(jnp.int32, (chunk, 2 * wide), 0).astype(F32).astype(BF16)

    blocks = n_col // 4

    def one_column(step, carry):
        q = lax.rem(step, n_row) * blocks + lax.div(step, n_row)
        for sent, mine in ((3, q == 0), (4, q > 0)):
            @pl.when(mine)
            def _():
                await_some(idx_all, sent, idx_recv.at[q])
        s = flip(lax.div(me, 4), q, count // 4)
        wanted = jnp.concatenate(
            [jnp.maximum(idx_all[4 * s + i], idx_all[4 * s + i + 1]) for i in (0, 2)], axis=1
        )

        which = jnp.right_shift(wanted, chunk.bit_length() - 1)
        offset = jnp.bitwise_and(wanted, chunk - 1).astype(F32).astype(BF16)
        picks = jnp.where(small == offset, jnp.ones_like(small), jnp.zeros_like(small))

        if chunks <= 8:
            taken = dot(coarse_split[...], picks)
            acc = jnp.zeros((2 * part, 2 * wide), F32)
            for k in range(chunks):
                acc = jnp.where(which == k, taken[2 * part * k : 2 * part * (k + 1)], acc)
        else:

            def one_chunk(k, acc):
                rows = pl.ds(pl.multiple_of(2 * part * k, 2 * part), 2 * part)
                return jnp.where(which == k, dot(coarse_split[rows, :], picks), acc)

            acc = lax.fori_loop(0, chunks, one_chunk, jnp.zeros((2 * part, 2 * wide), F32))
        values = join(acc)
        top = values.astype(BF16)
        at = pl.ds(pl.multiple_of(s * 2 * wide, 2 * wide), 2 * wide)
        columns[:part, at] = top
        columns[half : half + part, at] = (values - top.astype(F32)).astype(BF16)
        return carry

    lax.fori_loop(0, count // 4, one_column, 0)

    def gathered(buffer):
        return split(
            jnp.concatenate([unpack(buffer[s], buffer[s + 1]) for s in range(0, count, 2)], axis=1)
        )

    arrive(val_all.at[0], RHS)
    solved = join(dot_nt(gathered(val_all.at[0]), columns[...]))
    solved = solved + pltpu.roll(solved, half, 1)
    val_all[1, me] = pack(solved)
    start(val_all.at[1], SOL)

    pl.when(early)(last_sweep)

    for slot in range(4):
        @pl.when(flags[slot])
        def _():
            near_copy(slot).wait_recv()

        @pl.when(jnp.logical_not(flags[slot]))
        def _():
            near_in[slot] = jnp.full(near_in.shape[1:], -1, jnp.int32)

    def inverse(order_hot):
        order = lax.broadcasted_iota(jnp.int32, (8, face), 1).astype(F32)
        return join(dot_nt(split(order), order_hot[...]))[:1]

    def in_turn(rows):
        joined = None
        for i, row in enumerate(rows):
            wide_place[...] = jnp.full(wide_place.shape, -1, jnp.int32)
            wide_place[:1, :lanes] = row
            row = wide_place[...]
            row = pltpu.roll(row, i * nprim, 1) if i else row
            joined = row if joined is None else jnp.maximum(joined, row)
        return joined[:1]

    west, east, south, north = [near_in[slot] for slot in range(4)]
    target = in_turn(
        [
            numbers,
            look_up(inverse(west_hot), west[1:2] - face, 0),
            east[2:3],
            look_up(inverse(south_hot), south[1:2] - 3 * face, 2 * face),
            north[3:4],
        ]
    )
    wanted_coarse = in_turn([near_out[:1, :]] + [near[:1] for near in (west, east, south, north)])
    target = jnp.broadcast_to(target.astype(F32), (8, five)).T[:, :1].astype(jnp.int32)
    place_hot[...] = jnp.where(
        lax.broadcasted_iota(jnp.int32, (five, unknowns), 1) == target, weights, 0.0
    ).astype(BF16)
    spread = dot(place_hot[...], schur_hi[...]) + dot(place_hot[...], schur_lo[...])
    top = spread.astype(BF16)
    spread_hi[...] = top
    spread_lo[...] = (spread - top.astype(F32)).astype(BF16)

    at = lax.broadcasted_iota(jnp.int32, (wide, five), 0)
    upper = (at >= half).astype(jnp.int32)
    number = upper * coarse_rows + at - upper * half
    number = jnp.where(at - upper * half < coarse_rows, number, -2 * coarse_all)

    def one_pick(s, carry):
        coarse_hot[pl.ds(pl.multiple_of(s * wide, wide), wide), :] = one_hot(
            number, wanted_coarse - s * 2 * coarse_rows
        )
        return carry

    lax.fori_loop(0, count // 2, one_pick, 0)
    before = face_finish(1, weights * local[...])
    image_before = apply(schur_hi, schur_lo, before)

    def lane_sum(values):
        return jnp.sum(values, axis=1, keepdims=True)

    arrive(val_all.at[1], SOL)
    read = split(join(dot(gathered(val_all.at[1]), coarse_hot[...])))
    precond = before + join(dot(read, place_hot[...]))
    image = image_before + join(dot(read, spread_hi[...]) + dot(read, spread_lo[...]))
    rz = lane_sum(scaled * precond)
    pq = lane_sum(precond * image)
    sum_lane = lax.broadcasted_iota(jnp.int32, (rhs, 128), 1)
    sum_case = lax.broadcasted_iota(jnp.int32, (rhs, 128), 0)
    upper_lane, lower_lane = sum_lane == sum_case + rhs, sum_lane == sum_case
    laid = jnp.where(lower_lane, rz, 0.0) + jnp.where(upper_lane, pq, 0.0)
    sum_all[me] = jnp.sum(laid, axis=0, keepdims=True)
    start(sum_all, SUM)
    face_fill(2, image)
    when_neighbour(can_send, lambda slot: face_copy(2, slot).start())
    direction[...] = precond
    loads_out[...] = right_side
    await_all(idx_all, idx_send)
    await_all(val_all.at[0], all_send.at[RHS])
    await_all(val_all.at[1], all_send.at[SOL])
    for turn in range(2):
        when_neighbour(can_send, lambda slot: face_copy(turn, slot).wait_send())
    when_neighbour(can_send, lambda slot: near_copy(slot).wait_send())
    image_out[...] = face_finish(2, image)
    arrive(sum_all, SUM)
    parts = [sum_all[i] for i in range(count)]
    while len(parts) > 1:
        parts = [x + y for x, y in zip(parts[::2], parts[1::2])]
    sums = jnp.broadcast_to(parts[0], (rhs, 128))
    alpha = lane_sum(jnp.where(lower_lane, sums, 0.0)) / lane_sum(jnp.where(upper_lane, sums, 0.0))
    alpha_out[...] = jnp.broadcast_to(alpha, alpha_out.shape)
    await_all(sum_all, all_send.at[SUM])
    when_neighbour(can_send, lambda slot: face_copy(2, slot).wait_send())


def up(n, to):
    return -(-n // to) * to


def body(
    n_row, n_col, loads, schur, factor, coarse_inverse, elements, west_map, south_map,
    prim_local, prim_coarse,
):
    vectors = loads[0, 0].T
    rhs, unknowns = vectors.shape
    face = unknowns // 4
    coarse_rows, coarse_all = coarse_inverse.shape
    nprim = prim_local.shape[2]
    wide = 2 * up(max(nprim, coarse_rows), 64)
    count = n_row * n_col
    lanes, five = up(nprim, 128), up(5 * nprim, 128)
    vmem = pl.BlockSpec(memory_space=pltpu.VMEM)
    hbm = pl.BlockSpec(memory_space=pl.ANY)
    dma = pltpu.SemaphoreType.DMA
    out = pltpu.VMEM(vectors.shape, F32)
    direction, image, right_side, alpha = pl.pallas_call(
        functools.partial(kernel, n_row, n_col),
        out_shape=(out, out, out, out),
        in_specs=[hbm] * 9,
        out_specs=(vmem, vmem, vmem, vmem),
        scratch_shapes=[
            pltpu.VMEM(vectors.shape, F32),
            pltpu.VMEM((1, 1), jnp.int32),
            pltpu.VMEM((1, face), jnp.int32),
            pltpu.VMEM((1, face), jnp.int32),
            pltpu.VMEM((1, nprim), jnp.int32),
            pltpu.VMEM((1, nprim), jnp.int32),
            pltpu.VMEM((unknowns, unknowns), F32),
            pltpu.VMEM((unknowns, unknowns), F32),
            pltpu.VMEM((coarse_rows, coarse_all), F32),
            pltpu.VMEM((unknowns, unknowns), BF16),
            pltpu.VMEM((unknowns, unknowns), BF16),
            pltpu.VMEM((unknowns, unknowns), BF16),
            pltpu.VMEM((unknowns, unknowns), BF16),
            pltpu.VMEM((coarse_all // face * 2 * up(coarse_rows, 16), face), BF16),
            pltpu.VMEM((wide, count // 2 * wide), BF16),
            pltpu.VMEM((face, face), BF16),
            pltpu.VMEM((face, face), BF16),
            pltpu.VMEM((unknowns, wide), BF16),
            pltpu.VMEM((count // 2 * wide, five), BF16),
            pltpu.VMEM((five, unknowns), BF16),
            pltpu.VMEM((five, unknowns), BF16),
            pltpu.VMEM((five, unknowns), BF16),
            pltpu.VMEM(vectors.shape, F32),
            pltpu.VMEM((8, wide), jnp.int32),
            pltpu.VMEM((8, five), jnp.int32),
            pltpu.VMEM((count, 1, wide), jnp.int32),
            pltpu.VMEM((2, count, rhs // 2, wide), F32),
            pltpu.VMEM((count, 1, 128), F32),
            pltpu.VMEM((3, 4, rhs, face), F32),
            pltpu.VMEM((3, 4, rhs, face), F32),
            pltpu.VMEM((4, lanes), jnp.int32),
            pltpu.VMEM((4, 4, lanes), jnp.int32),
            dma((9,)),
            dma((3, 4)),
            dma((3, 4)),
            dma((4,)),
            dma((4,)),
            dma(()),
            dma((count // 4,)),
            dma((3,)),
            dma((3,)),
            pltpu.SemaphoreType.REGULAR,
        ],
        compiler_params=pltpu.CompilerParams(collective_id=0, has_side_effects=True),
    )(
        vectors, schur[0, 0], factor[0, 0], coarse_inverse, elements,
        west_map[0], south_map[0], prim_local[0], prim_coarse[0],
    )
    solution = alpha * direction
    residual = right_side - alpha * image
    return solution.T[None, None], residual.T[None, None]


def solution(mesh):
    placed = (
        P("row", "col", None, None),
        P("row", "col", None, None),
        P("row", "col", None, None),
        P(("row", "col"), None),
        P("row", "col"),
        P("row", "col", None),
        P("row", "col", None),
        P("row", "col", None),
        P("row", "col", None),
    )
    return jax.shard_map(
        functools.partial(body, mesh.shape["row"], mesh.shape["col"]),
        mesh=mesh,
        in_specs=placed,
        out_specs=(P("row", "col", None, None), P("row", "col", None, None)),
        check_vma=False,
    )
```

```python
import functools

import jax
import jax.numpy as jnp
from jax import lax
from jax.experimental import pallas as pl
from jax.experimental.pallas import tpu as pltpu
from jax.sharding import PartitionSpec as P

ELEM_BASE = 4096
MOST_SWEEPS = 3
MESH = pl.DeviceIdType.MESH
F32, BF16 = jnp.float32, jnp.bfloat16
NT = (((1,), (1,)), ((), ()))
RHS, SOL, SUM = range(3)


def split(values):
    high = values.astype(BF16).astype(F32)
    return jnp.concatenate([high, values - high], axis=0).astype(BF16)


def join(stacked):
    rows = stacked.shape[0] // 2
    return stacked[:rows] + stacked[rows:]


def one_hot(numbers, wanted):
    return jnp.where(numbers == wanted, 1.0, 0.0).astype(BF16)


def dot(a, b):
    return jnp.dot(a, b, preferred_element_type=F32)


def dot_nt(a, b):
    return lax.dot_general(a, b, NT, preferred_element_type=F32)


def flip(value, mask, size):
    out, weight = 0, 1
    while weight < size:
        bit = lax.rem(lax.div(value, weight), 2)
        if isinstance(mask, int):
            bit = 1 - bit if (mask // weight) % 2 else bit
        else:
            bit = lax.rem(bit + lax.rem(lax.div(mask, weight), 2), 2)
        out, weight = out + weight * bit, 2 * weight
    return out


def kernel(
    n_row, n_col, loads_hbm, schur_hbm, factor_hbm, coarse_hbm, elements_hbm, west_hbm, south_hbm,
    local_hbm, prim_hbm, direction, image_out, loads_out, alpha_out,
    loads, elements, west_map, south_map, prim_local, prim_coarse,
    schur_in, factor_in, coarse_in, schur_hi, schur_lo, factor_hi, factor_lo,
    coarse_split, columns, west_hot, south_hot, local_hot, coarse_hot, place_hot, spread_hi, spread_lo, local,
    place, wide_place, idx_all, val_all, sum_all, face_out, face_in, near_out, near_in,
    copy_sem, face_send, face_recv, near_send, near_recv, idx_send, idx_recv, all_send, all_recv, entered,
):
    a, c = lax.axis_index("row"), lax.axis_index("col")
    unknowns = loads.shape[1]
    face = unknowns // 4
    wide = local_hot.shape[1]
    half = wide // 2
    count = n_row * n_col
    me = a * n_col + c
    spot = c * n_row + a
    odd = lax.rem(a, 2)
    coarse_rows, coarse_all = coarse_in.shape
    nprim = prim_local.shape[1]
    lanes = near_out.shape[1]
    five = place_hot.shape[0]

    copies = [
        pltpu.make_async_copy(src, dst, copy_sem.at[i])
        for i, (src, dst) in enumerate(
            [
                (factor_hbm, factor_in), (coarse_hbm, coarse_in), (schur_hbm, schur_in),
                (loads_hbm, loads), (west_hbm, west_map), (south_hbm, south_map),
                (local_hbm, prim_local), (prim_hbm, prim_coarse), (elements_hbm, elements),
            ]
        )
    ]
    barrier = pltpu.get_barrier_semaphore()
    column_mates = [(flip(a, m, n_row), c) for m in range(1, n_row)]
    row_mates = [(a, flip(c, m, n_col)) for m in range(1, n_col)]
    for mate in row_mates + column_mates:
        pl.semaphore_signal(barrier, inc=1, device_id=mate, device_id_type=MESH)
    for copy in copies[3:] + copies[:3]:
        copy.start()

    rows_of = [flip(a, m, n_row) for m in range(n_row)]
    cols_of = [flip(c, m, n_col) for m in range(n_col)]

    def peer(m):
        if not isinstance(m, int):
            return (flip(a, lax.div(m, n_col), n_row), flip(c, lax.rem(m, n_col), n_col))
        return (rows_of[m // n_col], cols_of[m % n_col])

    def each(work):
        if count <= 64:
            for m in range(count - 1, 0, -1):
                work(m)
        else:
            lax.fori_loop(1, count, lambda d, carry: (work(count - d), carry)[1], 0)

    for copy in copies[3:]:
        copy.wait()

    def hot(order_ref):
        return one_hot(lax.broadcasted_iota(jnp.int32, (face, face), 0), order_ref[...])

    west_hot[...] = hot(west_map)
    south_hot[...] = hot(south_map)

    lane = lax.broadcasted_iota(jnp.int32, (1, unknowns), 1)
    flags = [c > 0, c < n_col - 1, a > 0, a < n_row - 1]
    halves = [jnp.where(flag, 0.5, 1.0).astype(F32) for flag in flags]
    weights = jnp.where(
        lane < face,
        halves[0],
        jnp.where(lane < 2 * face, halves[1], jnp.where(lane < 3 * face, halves[2], halves[3])),
    )
    targets = [(a, c + 1), (a, c - 1), (a + 1, c), (a - 1, c)]
    can_send = [flags[1], flags[0], flags[3], flags[2]]

    def face_copy(turn, slot):
        return pltpu.make_async_remote_copy(
            src_ref=face_out.at[turn, slot],
            dst_ref=face_in.at[turn, slot],
            send_sem=face_send.at[turn, slot],
            recv_sem=face_recv.at[turn, slot],
            device_id=targets[slot],
            device_id_type=MESH,
        )

    def near_copy(slot):
        return pltpu.make_async_remote_copy(
            src_ref=near_out,
            dst_ref=near_in.at[slot],
            send_sem=near_send.at[slot],
            recv_sem=near_recv.at[slot],
            device_id=targets[slot],
            device_id_type=MESH,
        )

    def face_fill(turn, values):
        face_out[turn, 0] = values[:, face : 2 * face]
        face_out[turn, 2] = values[:, 3 * face :]
        face_out[turn, 1] = join(dot_nt(split(values[:, :face]), west_hot[...]))
        face_out[turn, 3] = join(dot_nt(split(values[:, 2 * face : 3 * face]), south_hot[...]))

    def when_neighbour(present, work):
        for slot in range(4):
            @pl.when(present[slot])
            def _():
                work(slot)

    def face_finish(turn, values):
        for slot in range(4):
            @pl.when(flags[slot])
            def _():
                face_copy(turn, slot).wait_recv()

            @pl.when(jnp.logical_not(flags[slot]))
            def _():
                face_in[turn, slot] = jnp.zeros(face_in.shape[2:], F32)
        adds = [
            join(dot(split(face_in[turn, 0]), west_hot[...])),
            face_in[turn, 1],
            join(dot(split(face_in[turn, 2]), south_hot[...])),
            face_in[turn, 3],
        ]
        return values + jnp.concatenate(adds, axis=1)

    def column_copy(m):
        return pltpu.make_async_remote_copy(
            src_ref=idx_all.at[spot],
            dst_ref=idx_all.at[spot],
            send_sem=idx_send.at[0],
            recv_sem=idx_recv.at[0],
            device_id=column_mates[m - 1],
            device_id_type=MESH,
        )

    def row_copy(m):
        own = idx_all.at[pl.ds(c * n_row, n_row)]
        return pltpu.make_async_remote_copy(
            src_ref=own,
            dst_ref=own,
            send_sem=idx_send.at[1],
            recv_sem=idx_recv.at[m],
            device_id=(a, cols_of[m] if isinstance(m, int) else flip(c, m, n_col)),
            device_id_type=MESH,
        )

    first = loads[...]
    face_fill(0, first)
    pl.semaphore_wait(barrier, n_row + n_col - 2)
    for mate in column_mates:
        pl.semaphore_signal(entered, inc=1, device_id=mate, device_id_type=MESH)
    when_neighbour(can_send, lambda slot: face_copy(0, slot).start())

    def placed(source):
        place[...] = jnp.full(place.shape, -1, jnp.int32)
        place[:1, :nprim] = source[...]
        base = place[...]
        return base, pltpu.roll(base, half, 1)

    base, rolled = placed(prim_coarse)
    own_coarse = jnp.where(odd == 1, rolled, base)[:1]
    idx_all[spot] = own_coarse
    for m in range(1, n_row):
        column_copy(m).start()
    near_out[...] = jnp.full(near_out.shape, -1, jnp.int32)
    near_out[:1, :nprim] = prim_coarse[...]
    near_out[1:2, :nprim] = prim_local[...]
    numbers = near_out[1:2, :]
    depth = lax.broadcasted_iota(jnp.int32, (face, lanes), 0)

    def look_up(table, numbers, offset):
        inside = jnp.logical_and(numbers >= 0, numbers < face)
        table = jnp.broadcast_to(table, (8, face)).astype(F32)
        found = join(dot(split(table), one_hot(depth, numbers)))[:1]
        return jnp.where(inside, found.astype(jnp.int32) + offset, -1)

    near_out[2:3, :] = look_up(west_map[...], numbers, face)
    near_out[3:4, :] = look_up(south_map[...], numbers - 2 * face, 3 * face)
    when_neighbour(can_send, lambda slot: near_copy(slot).start())

    own_local = jnp.maximum(*placed(prim_local))[:1]
    rows_iota = lax.broadcasted_iota(jnp.int32, (unknowns, wide), 0)
    local_hot[...] = one_hot(rows_iota, own_local)

    def all_copy(buffer, kind, m):
        return pltpu.make_async_remote_copy(
            src_ref=buffer.at[spot if kind == RHS else me],
            dst_ref=buffer.at[spot if kind == RHS else me],
            send_sem=all_send.at[kind],
            recv_sem=all_recv.at[kind],
            device_id=peer(m),
            device_id_type=MESH,
        )

    def start(buffer, kind):
        each(lambda m: all_copy(buffer, kind, m).start())

    def await_some(buffer, sent, semaphore):
        slots = buffer.at[pl.ds(0, sent)]
        pltpu.make_async_copy(slots, slots, semaphore).wait()

    def await_all(buffer, semaphore):
        await_some(buffer, count - 1, semaphore)

    def arrive(buffer, kind):
        await_all(buffer, all_recv.at[kind])

    rhs = loads.shape[0]
    lower = lax.broadcasted_iota(jnp.int32, (rhs // 2, wide), 1) < half

    def pack(values):
        return jnp.where(lower, values[: rhs // 2], values[rhs // 2 :])

    square = (rhs, wide)
    stays = (lax.broadcasted_iota(jnp.int32, square, 1) < half) == (
        lax.broadcasted_iota(jnp.int32, square, 0) < rhs // 2
    )

    def unpack(first, second):
        both = jnp.concatenate([first, second], axis=0)
        return jnp.where(stays, both, pltpu.roll(pltpu.roll(both, half, 1), rhs // 2, 0))

    def split_matrix(source, high, low):
        step = 128

        def one(i, carry):
            at = pl.ds(pl.multiple_of(i * step, step), step)
            values = source[at, :]
            top = values.astype(BF16)
            high[at, :] = top
            low[at, :] = (values - top.astype(F32)).astype(BF16)
            return carry

        lax.fori_loop(0, source.shape[0] // step, one, 0)

    chunk = coarse_split.shape[1]
    chunks = coarse_all // chunk
    part = coarse_split.shape[0] // chunks // 2

    def over_chunks(work, carry):
        if chunks <= 8:
            for k in range(chunks):
                carry = work(k, carry)
            return carry
        return lax.fori_loop(0, chunks, work, carry)

    def split_coarse():
        copies[1].wait()
        columns[...] = jnp.zeros(columns.shape, BF16)
        if coarse_rows < part:
            coarse_split[...] = jnp.zeros(coarse_split.shape, BF16)

        def one(k, carry):
            at = k * chunk if isinstance(k, int) else pl.multiple_of(k * chunk, chunk)
            rows = 2 * part * k if isinstance(k, int) else pl.multiple_of(2 * part * k, 2 * part)
            values = coarse_in[:, pl.ds(at, chunk)]
            top = values.astype(BF16)
            coarse_split[pl.ds(rows, coarse_rows), :] = top
            coarse_split[pl.ds(rows + part, coarse_rows), :] = (values - top.astype(F32)).astype(BF16)
            return carry

        over_chunks(one, 0)

    early = c < n_col // 2

    def split_schur():
        copies[2].wait()
        split_matrix(schur_in, schur_hi, schur_lo)

    copies[0].wait()
    split_matrix(factor_in, factor_hi, factor_lo)
    split_coarse()
    pl.when(early)(split_schur)
    right_side = face_finish(0, first)
    scaled = weights * right_side
    val_all[0, spot] = pack(join(dot(split(scaled), local_hot[...])))
    await_some(idx_all, n_row - 1, idx_recv.at[0])
    pl.semaphore_wait(entered, n_row - 1)
    start(val_all.at[0], RHS)
    for m in range(1, n_col):
        row_copy(m).start()

    def apply(high, low, vectors):
        both = split(vectors)
        return join(dot(both, high[...]) + dot(both, low[...]))

    pl.when(jnp.logical_not(early))(split_schur)
    local[...] = apply(factor_hi, factor_lo, scaled)

    def sweep(turn):
        now = local[...]
        inner = scaled - apply(schur_hi, schur_lo, now)
        later = now + apply(factor_hi, factor_lo, inner)
        more = jnp.broadcast_to(elements[...], now.shape) >= turn * ELEM_BASE
        local[...] = jnp.where(more, later, now)

    def last_sweep():
        sweep(MOST_SWEEPS)
        face_fill(1, weights * local[...])
        when_neighbour(can_send, lambda slot: face_copy(1, slot).start())

    for turn in range(2, MOST_SWEEPS):
        sweep(turn)
    pl.when(jnp.logical_not(early))(last_sweep)

    group = 8
    span = group // 2 * wide
    small = lax.broadcasted_iota(jnp.int32, (chunk, span), 0).astype(F32).astype(BF16)
    cols_each, blocks = max(1, group // n_row), max(1, n_row // group)

    def one_column(step, carry):
        k = lax.div(step, blocks)
        for i in range(cols_each):
            q = k * cols_each + i

            @pl.when(jnp.logical_and(q > 0, lax.rem(step, blocks) == 0))
            def _():
                row_copy(q).wait_recv()

        s = flip(lax.div(c, cols_each), k, n_col // cols_each) * blocks + lax.rem(step, blocks)
        wanted = jnp.concatenate(
            [
                jnp.maximum(idx_all[group * s + i], idx_all[group * s + i + 1])
                for i in range(0, group, 2)
            ],
            axis=1,
        )
        which = jnp.right_shift(wanted, chunk.bit_length() - 1)
        offset = jnp.bitwise_and(wanted, chunk - 1).astype(F32).astype(BF16)
        picks = jnp.where(small == offset, jnp.ones_like(small), jnp.zeros_like(small))

        if chunks <= 8:
            taken = dot(coarse_split[...], picks)
            acc = jnp.zeros((2 * part, span), F32)
            for k in range(chunks):
                acc = jnp.where(which == k, taken[2 * part * k : 2 * part * (k + 1)], acc)
        else:

            def one_chunk(k, acc):
                rows = pl.ds(pl.multiple_of(2 * part * k, 2 * part), 2 * part)
                return jnp.where(which == k, dot(coarse_split[rows, :], picks), acc)

            acc = lax.fori_loop(0, chunks, one_chunk, jnp.zeros((2 * part, span), F32))
        values = join(acc)
        top = values.astype(BF16)
        at = pl.ds(pl.multiple_of(s * span, span), span)
        columns[:part, at] = top
        columns[half : half + part, at] = (values - top.astype(F32)).astype(BF16)
        return carry

    lax.fori_loop(0, count // group, one_column, 0)

    def gathered(buffer):
        return split(
            jnp.concatenate([unpack(buffer[s], buffer[s + 1]) for s in range(0, count, 2)], axis=1)
        )

    arrive(val_all.at[0], RHS)
    solved = join(dot_nt(gathered(val_all.at[0]), columns[...]))
    solved = solved + pltpu.roll(solved, half, 1)
    val_all[1, me] = pack(solved)
    start(val_all.at[1], SOL)

    pl.when(early)(last_sweep)

    for slot in range(4):
        @pl.when(flags[slot])
        def _():
            near_copy(slot).wait_recv()

        @pl.when(jnp.logical_not(flags[slot]))
        def _():
            near_in[slot] = jnp.full(near_in.shape[1:], -1, jnp.int32)

    def inverse(order_hot):
        order = lax.broadcasted_iota(jnp.int32, (8, face), 1).astype(F32)
        return join(dot_nt(split(order), order_hot[...]))[:1]

    def in_turn(rows):
        joined = None
        for i, row in enumerate(rows):
            wide_place[...] = jnp.full(wide_place.shape, -1, jnp.int32)
            wide_place[:1, :lanes] = row
            row = wide_place[...]
            row = pltpu.roll(row, i * nprim, 1) if i else row
            joined = row if joined is None else jnp.maximum(joined, row)
        return joined[:1]

    west, east, south, north = [near_in[slot] for slot in range(4)]
    target = in_turn(
        [
            numbers,
            look_up(inverse(west_hot), west[1:2] - face, 0),
            east[2:3],
            look_up(inverse(south_hot), south[1:2] - 3 * face, 2 * face),
            north[3:4],
        ]
    )
    wanted_coarse = in_turn([near_out[:1, :]] + [near[:1] for near in (west, east, south, north)])
    target = jnp.broadcast_to(target.astype(F32), (8, five)).T[:, :1].astype(jnp.int32)
    place_hot[...] = jnp.where(
        lax.broadcasted_iota(jnp.int32, (five, unknowns), 1) == target, weights, 0.0
    ).astype(BF16)
    spread = dot(place_hot[...], schur_hi[...]) + dot(place_hot[...], schur_lo[...])
    top = spread.astype(BF16)
    spread_hi[...] = top
    spread_lo[...] = (spread - top.astype(F32)).astype(BF16)

    at = lax.broadcasted_iota(jnp.int32, (wide, five), 0)
    upper = (at >= half).astype(jnp.int32)
    number = upper * coarse_rows + at - upper * half
    number = jnp.where(at - upper * half < coarse_rows, number, -2 * coarse_all)

    def one_pick(s, carry):
        coarse_hot[pl.ds(pl.multiple_of(s * wide, wide), wide), :] = one_hot(
            number, wanted_coarse - s * 2 * coarse_rows
        )
        return carry

    lax.fori_loop(0, count // 2, one_pick, 0)
    before = face_finish(1, weights * local[...])
    image_before = apply(schur_hi, schur_lo, before)

    def lane_sum(values):
        return jnp.sum(values, axis=1, keepdims=True)

    arrive(val_all.at[1], SOL)
    read = split(join(dot(gathered(val_all.at[1]), coarse_hot[...])))
    precond = before + join(dot(read, place_hot[...]))
    image = image_before + join(dot(read, spread_hi[...]) + dot(read, spread_lo[...]))
    rz = lane_sum(scaled * precond)
    pq = lane_sum(precond * image)
    sum_lane = lax.broadcasted_iota(jnp.int32, (rhs, 128), 1)
    sum_case = lax.broadcasted_iota(jnp.int32, (rhs, 128), 0)
    upper_lane, lower_lane = sum_lane == sum_case + rhs, sum_lane == sum_case
    laid = jnp.where(lower_lane, rz, 0.0) + jnp.where(upper_lane, pq, 0.0)
    sum_all[me] = jnp.sum(laid, axis=0, keepdims=True)
    start(sum_all, SUM)
    face_fill(2, image)
    when_neighbour(can_send, lambda slot: face_copy(2, slot).start())
    direction[...] = precond
    loads_out[...] = right_side
    await_some(idx_all, n_row - 1, idx_send.at[0])
    await_some(idx_all, n_row * (n_col - 1), idx_send.at[1])
    await_all(val_all.at[0], all_send.at[RHS])
    await_all(val_all.at[1], all_send.at[SOL])
    for turn in range(2):
        when_neighbour(can_send, lambda slot: face_copy(turn, slot).wait_send())
    when_neighbour(can_send, lambda slot: near_copy(slot).wait_send())
    image_out[...] = face_finish(2, image)
    arrive(sum_all, SUM)
    parts = [sum_all[i] for i in range(count)]
    while len(parts) > 1:
        parts = [x + y for x, y in zip(parts[::2], parts[1::2])]
    sums = jnp.broadcast_to(parts[0], (rhs, 128))
    alpha = lane_sum(jnp.where(lower_lane, sums, 0.0)) / lane_sum(jnp.where(upper_lane, sums, 0.0))
    alpha_out[...] = jnp.broadcast_to(alpha, alpha_out.shape)
    await_all(sum_all, all_send.at[SUM])
    when_neighbour(can_send, lambda slot: face_copy(2, slot).wait_send())


def up(n, to):
    return -(-n // to) * to


def body(
    n_row, n_col, loads, schur, factor, coarse_inverse, elements, west_map, south_map,
    prim_local, prim_coarse,
):
    vectors = loads[0, 0].T
    rhs, unknowns = vectors.shape
    face = unknowns // 4
    coarse_rows, coarse_all = coarse_inverse.shape
    nprim = prim_local.shape[2]
    wide = 2 * up(max(nprim, coarse_rows), 64)
    count = n_row * n_col
    lanes, five = up(nprim, 128), up(5 * nprim, 128)
    vmem = pl.BlockSpec(memory_space=pltpu.VMEM)
    hbm = pl.BlockSpec(memory_space=pl.ANY)
    dma = pltpu.SemaphoreType.DMA
    out = pltpu.VMEM(vectors.shape, F32)
    direction, image, right_side, alpha = pl.pallas_call(
        functools.partial(kernel, n_row, n_col),
        out_shape=(out, out, out, out),
        in_specs=[hbm] * 9,
        out_specs=(vmem, vmem, vmem, vmem),
        scratch_shapes=[
            pltpu.VMEM(vectors.shape, F32),
            pltpu.VMEM((1, 1), jnp.int32),
            pltpu.VMEM((1, face), jnp.int32),
            pltpu.VMEM((1, face), jnp.int32),
            pltpu.VMEM((1, nprim), jnp.int32),
            pltpu.VMEM((1, nprim), jnp.int32),
            pltpu.VMEM((unknowns, unknowns), F32),
            pltpu.VMEM((unknowns, unknowns), F32),
            pltpu.VMEM((coarse_rows, coarse_all), F32),
            pltpu.VMEM((unknowns, unknowns), BF16),
            pltpu.VMEM((unknowns, unknowns), BF16),
            pltpu.VMEM((unknowns, unknowns), BF16),
            pltpu.VMEM((unknowns, unknowns), BF16),
            pltpu.VMEM((coarse_all // face * 2 * up(coarse_rows, 16), face), BF16),
            pltpu.VMEM((wide, count // 2 * wide), BF16),
            pltpu.VMEM((face, face), BF16),
            pltpu.VMEM((face, face), BF16),
            pltpu.VMEM((unknowns, wide), BF16),
            pltpu.VMEM((count // 2 * wide, five), BF16),
            pltpu.VMEM((five, unknowns), BF16),
            pltpu.VMEM((five, unknowns), BF16),
            pltpu.VMEM((five, unknowns), BF16),
            pltpu.VMEM(vectors.shape, F32),
            pltpu.VMEM((8, wide), jnp.int32),
            pltpu.VMEM((8, five), jnp.int32),
            pltpu.VMEM((count, 1, wide), jnp.int32),
            pltpu.VMEM((2, count, rhs // 2, wide), F32),
            pltpu.VMEM((count, 1, 128), F32),
            pltpu.VMEM((3, 4, rhs, face), F32),
            pltpu.VMEM((3, 4, rhs, face), F32),
            pltpu.VMEM((4, lanes), jnp.int32),
            pltpu.VMEM((4, 4, lanes), jnp.int32),
            dma((9,)),
            dma((3, 4)),
            dma((3, 4)),
            dma((4,)),
            dma((4,)),
            dma((2,)),
            dma((n_col,)),
            dma((3,)),
            dma((3,)),
            pltpu.SemaphoreType.REGULAR,
        ],
        compiler_params=pltpu.CompilerParams(collective_id=0, has_side_effects=True),
    )(
        vectors, schur[0, 0], factor[0, 0], coarse_inverse, elements,
        west_map[0], south_map[0], prim_local[0], prim_coarse[0],
    )
    solution = alpha * direction
    residual = right_side - alpha * image
    return solution.T[None, None], residual.T[None, None]


def solution(mesh):
    placed = (
        P("row", "col", None, None),
        P("row", "col", None, None),
        P("row", "col", None, None),
        P(("row", "col"), None),
        P("row", "col"),
        P("row", "col", None),
        P("row", "col", None),
        P("row", "col", None),
        P("row", "col", None),
    )
    return jax.shard_map(
        functools.partial(body, mesh.shape["row"], mesh.shape["col"]),
        mesh=mesh,
        in_specs=placed,
        out_specs=(P("row", "col", None, None), P("row", "col", None, None)),
        check_vma=False,
    )
```

```python
import functools

import jax
import jax.numpy as jnp
from jax import lax
from jax.experimental import pallas as pl
from jax.experimental.pallas import tpu as pltpu
from jax.sharding import PartitionSpec as P

ELEM_BASE = 4096
MOST_SWEEPS = 3
MESH = pl.DeviceIdType.MESH
F32, BF16 = jnp.float32, jnp.bfloat16
NT = (((1,), (1,)), ((), ()))
RHS, SOL, SUM = range(3)


def split(values):
    high = values.astype(BF16).astype(F32)
    return jnp.concatenate([high, values - high], axis=0).astype(BF16)


def join(stacked):
    rows = stacked.shape[0] // 2
    return stacked[:rows] + stacked[rows:]


def one_hot(numbers, wanted):
    return jnp.where(numbers == wanted, 1.0, 0.0).astype(BF16)


def dot(a, b):
    return jnp.dot(a, b, preferred_element_type=F32)


def dot_nt(a, b):
    return lax.dot_general(a, b, NT, preferred_element_type=F32)


def flip(value, mask, size):
    out, weight = 0, 1
    while weight < size:
        bit = lax.rem(lax.div(value, weight), 2)
        if isinstance(mask, int):
            bit = 1 - bit if (mask // weight) % 2 else bit
        else:
            bit = lax.rem(bit + lax.rem(lax.div(mask, weight), 2), 2)
        out, weight = out + weight * bit, 2 * weight
    return out


def kernel(
    n_row, n_col, loads_hbm, schur_hbm, factor_hbm, coarse_hbm, elements_hbm, west_hbm, south_hbm,
    local_hbm, prim_hbm, direction, image_out, loads_out, alpha_out,
    loads, elements, west_map, south_map, prim_local, prim_coarse,
    schur_in, factor_in, coarse_in, schur_hi, schur_lo, factor_hi, factor_lo,
    coarse_split, columns, west_hot, south_hot, local_hot, coarse_hot, place_hot, spread_hi, spread_lo, local,
    place, wide_place, idx_all, val_all, sum_all, face_out, face_in, near_out, near_in,
    copy_sem, face_send, face_recv, near_send, near_recv, idx_send, idx_recv, all_send, all_recv, entered,
):
    a, c = lax.axis_index("row"), lax.axis_index("col")
    unknowns = loads.shape[1]
    face = unknowns // 4
    wide = local_hot.shape[1]
    half = wide // 2
    count = n_row * n_col
    me = a * n_col + c
    spot = c * n_row + a
    odd = lax.rem(a, 2)
    coarse_rows, coarse_all = coarse_in.shape
    nprim = prim_local.shape[1]
    lanes = near_out.shape[1]
    five = place_hot.shape[0]

    copies = [
        pltpu.make_async_copy(src, dst, copy_sem.at[i])
        for i, (src, dst) in enumerate(
            [
                (factor_hbm, factor_in), (coarse_hbm, coarse_in), (schur_hbm, schur_in),
                (loads_hbm, loads), (west_hbm, west_map), (south_hbm, south_map),
                (local_hbm, prim_local), (prim_hbm, prim_coarse), (elements_hbm, elements),
            ]
        )
    ]
    barrier = pltpu.get_barrier_semaphore()
    column_mates = [(flip(a, m, n_row), c) for m in range(1, n_row)]
    row_mates = [(a, flip(c, m, n_col)) for m in range(1, n_col)]
    for mate in row_mates + column_mates:
        pl.semaphore_signal(barrier, inc=1, device_id=mate, device_id_type=MESH)
    for copy in copies[3:] + copies[:3]:
        copy.start()

    rows_of = [flip(a, m, n_row) for m in range(n_row)]
    cols_of = [flip(c, m, n_col) for m in range(n_col)]

    def peer(m):
        if not isinstance(m, int):
            return (flip(a, lax.div(m, n_col), n_row), flip(c, lax.rem(m, n_col), n_col))
        return (rows_of[m // n_col], cols_of[m % n_col])

    def each(work):
        if count <= 64:
            for m in range(count - 1, 0, -1):
                work(m)
        else:
            lax.fori_loop(1, count, lambda d, carry: (work(count - d), carry)[1], 0)

    for copy in copies[3:]:
        copy.wait()

    def hot(order_ref):
        return one_hot(lax.broadcasted_iota(jnp.int32, (face, face), 0), order_ref[...])

    west_hot[...] = hot(west_map)
    south_hot[...] = hot(south_map)

    lane = lax.broadcasted_iota(jnp.int32, (1, unknowns), 1)
    flags = [c > 0, c < n_col - 1, a > 0, a < n_row - 1]
    halves = [jnp.where(flag, 0.5, 1.0).astype(F32) for flag in flags]
    weights = jnp.where(
        lane < face,
        halves[0],
        jnp.where(lane < 2 * face, halves[1], jnp.where(lane < 3 * face, halves[2], halves[3])),
    )
    targets = [(a, c + 1), (a, c - 1), (a + 1, c), (a - 1, c)]
    can_send = [flags[1], flags[0], flags[3], flags[2]]

    def face_copy(turn, slot):
        return pltpu.make_async_remote_copy(
            src_ref=face_out.at[turn, slot],
            dst_ref=face_in.at[turn, slot],
            send_sem=face_send.at[turn, slot],
            recv_sem=face_recv.at[turn, slot],
            device_id=targets[slot],
            device_id_type=MESH,
        )

    def near_copy(slot):
        return pltpu.make_async_remote_copy(
            src_ref=near_out,
            dst_ref=near_in.at[slot],
            send_sem=near_send.at[slot],
            recv_sem=near_recv.at[slot],
            device_id=targets[slot],
            device_id_type=MESH,
        )

    def face_fill(turn, values):
        face_out[turn, 0] = values[:, face : 2 * face]
        face_out[turn, 2] = values[:, 3 * face :]
        face_out[turn, 1] = join(dot_nt(split(values[:, :face]), west_hot[...]))
        face_out[turn, 3] = join(dot_nt(split(values[:, 2 * face : 3 * face]), south_hot[...]))

    def when_neighbour(present, work):
        for slot in range(4):
            @pl.when(present[slot])
            def _():
                work(slot)

    def face_finish(turn, values):
        for slot in range(4):
            @pl.when(flags[slot])
            def _():
                face_copy(turn, slot).wait_recv()

            @pl.when(jnp.logical_not(flags[slot]))
            def _():
                face_in[turn, slot] = jnp.zeros(face_in.shape[2:], F32)
        adds = [
            join(dot(split(face_in[turn, 0]), west_hot[...])),
            face_in[turn, 1],
            join(dot(split(face_in[turn, 2]), south_hot[...])),
            face_in[turn, 3],
        ]
        return values + jnp.concatenate(adds, axis=1)

    def column_copy(m):
        return pltpu.make_async_remote_copy(
            src_ref=idx_all.at[spot],
            dst_ref=idx_all.at[spot],
            send_sem=idx_send.at[0],
            recv_sem=idx_recv.at[0],
            device_id=column_mates[m - 1],
            device_id_type=MESH,
        )

    def row_copy(m):
        own = idx_all.at[pl.ds(c * n_row, n_row)]
        return pltpu.make_async_remote_copy(
            src_ref=own,
            dst_ref=own,
            send_sem=idx_send.at[1],
            recv_sem=idx_recv.at[m],
            device_id=(a, cols_of[m] if isinstance(m, int) else flip(c, m, n_col)),
            device_id_type=MESH,
        )

    first = loads[...]
    face_fill(0, first)
    pl.semaphore_wait(barrier, n_row + n_col - 2)
    for mate in column_mates:
        pl.semaphore_signal(entered, inc=1, device_id=mate, device_id_type=MESH)
    when_neighbour(can_send, lambda slot: face_copy(0, slot).start())

    def placed(source):
        place[...] = jnp.full(place.shape, -1, jnp.int32)
        place[:1, :nprim] = source[...]
        base = place[...]
        return base, pltpu.roll(base, half, 1)

    base, rolled = placed(prim_coarse)
    own_coarse = jnp.where(odd == 1, rolled, base)[:1]
    idx_all[spot] = own_coarse
    for m in range(1, n_row):
        column_copy(m).start()
    near_out[...] = jnp.full(near_out.shape, -1, jnp.int32)
    near_out[:1, :nprim] = prim_coarse[...]
    near_out[1:2, :nprim] = prim_local[...]
    numbers = near_out[1:2, :]
    depth = lax.broadcasted_iota(jnp.int32, (face, lanes), 0)

    def look_up(table, numbers, offset):
        inside = jnp.logical_and(numbers >= 0, numbers < face)
        table = jnp.broadcast_to(table, (8, face)).astype(F32)
        found = join(dot(split(table), one_hot(depth, numbers)))[:1]
        return jnp.where(inside, found.astype(jnp.int32) + offset, -1)

    near_out[2:3, :] = look_up(west_map[...], numbers, face)
    near_out[3:4, :] = look_up(south_map[...], numbers - 2 * face, 3 * face)
    when_neighbour(can_send, lambda slot: near_copy(slot).start())

    own_local = jnp.maximum(*placed(prim_local))[:1]
    rows_iota = lax.broadcasted_iota(jnp.int32, (unknowns, wide), 0)
    local_hot[...] = one_hot(rows_iota, own_local)

    def all_copy(buffer, kind, m):
        return pltpu.make_async_remote_copy(
            src_ref=buffer.at[spot if kind == RHS else me],
            dst_ref=buffer.at[spot if kind == RHS else me],
            send_sem=all_send.at[kind],
            recv_sem=all_recv.at[kind],
            device_id=peer(m),
            device_id_type=MESH,
        )

    def start(buffer, kind):
        each(lambda m: all_copy(buffer, kind, m).start())

    def await_some(buffer, sent, semaphore):
        slots = buffer.at[pl.ds(0, sent)]
        pltpu.make_async_copy(slots, slots, semaphore).wait()

    def await_all(buffer, semaphore):
        await_some(buffer, count - 1, semaphore)

    def arrive(buffer, kind):
        await_all(buffer, all_recv.at[kind])

    rhs = loads.shape[0]
    lower = lax.broadcasted_iota(jnp.int32, (rhs // 2, wide), 1) < half

    def pack(values):
        return jnp.where(lower, values[: rhs // 2], values[rhs // 2 :])

    square = (rhs, wide)
    stays = (lax.broadcasted_iota(jnp.int32, square, 1) < half) == (
        lax.broadcasted_iota(jnp.int32, square, 0) < rhs // 2
    )

    def unpack(first, second):
        both = jnp.concatenate([first, second], axis=0)
        return jnp.where(stays, both, pltpu.roll(pltpu.roll(both, half, 1), rhs // 2, 0))

    def split_matrix(source, high, low):
        step = 128

        def one(i, carry):
            at = pl.ds(pl.multiple_of(i * step, step), step)
            values = source[at, :]
            top = values.astype(BF16)
            high[at, :] = top
            low[at, :] = (values - top.astype(F32)).astype(BF16)
            return carry

        lax.fori_loop(0, source.shape[0] // step, one, 0)

    chunk = coarse_split.shape[1]
    chunks = coarse_all // chunk
    part = coarse_split.shape[0] // chunks // 2

    def over_chunks(work, carry):
        if chunks <= 8:
            for k in range(chunks):
                carry = work(k, carry)
            return carry
        return lax.fori_loop(0, chunks, work, carry)

    def split_coarse():
        copies[1].wait()
        columns[...] = jnp.zeros(columns.shape, BF16)
        if coarse_rows < part:
            coarse_split[...] = jnp.zeros(coarse_split.shape, BF16)

        def one(k, carry):
            at = k * chunk if isinstance(k, int) else pl.multiple_of(k * chunk, chunk)
            rows = 2 * part * k if isinstance(k, int) else pl.multiple_of(2 * part * k, 2 * part)
            values = coarse_in[:, pl.ds(at, chunk)]
            top = values.astype(BF16)
            coarse_split[pl.ds(rows, coarse_rows), :] = top
            coarse_split[pl.ds(rows + part, coarse_rows), :] = (values - top.astype(F32)).astype(BF16)
            return carry

        over_chunks(one, 0)

    early = c < n_col // 2

    def split_schur():
        copies[2].wait()
        split_matrix(schur_in, schur_hi, schur_lo)

    copies[0].wait()
    split_matrix(factor_in, factor_hi, factor_lo)
    split_coarse()
    pl.when(early)(split_schur)
    right_side = face_finish(0, first)
    scaled = weights * right_side
    val_all[0, spot] = pack(join(dot(split(scaled), local_hot[...])))
    await_some(idx_all, n_row - 1, idx_recv.at[0])
    pl.semaphore_wait(entered, n_row - 1)
    start(val_all.at[0], RHS)
    for m in range(1, n_col):
        row_copy(m).start()

    def apply(high, low, vectors):
        both = split(vectors)
        return join(dot(both, high[...]) + dot(both, low[...]))

    pl.when(jnp.logical_not(early))(split_schur)
    local[...] = apply(factor_hi, factor_lo, scaled)

    def sweep(turn):
        now = local[...]
        inner = scaled - apply(schur_hi, schur_lo, now)
        later = now + apply(factor_hi, factor_lo, inner)
        more = jnp.broadcast_to(elements[...], now.shape) >= turn * ELEM_BASE
        local[...] = jnp.where(more, later, now)

    def last_sweep():
        sweep(MOST_SWEEPS)
        face_fill(1, weights * local[...])
        when_neighbour(can_send, lambda slot: face_copy(1, slot).start())

    for turn in range(2, MOST_SWEEPS):
        sweep(turn)
    pl.when(c >= n_col // 4)(last_sweep)

    group = 8
    span = group // 2 * wide
    small = lax.broadcasted_iota(jnp.int32, (chunk, span), 0).astype(F32).astype(BF16)
    cols_each, blocks = max(1, group // n_row), max(1, n_row // group)

    def one_column(step, carry):
        k = lax.div(step, blocks)
        for i in range(cols_each):
            q = k * cols_each + i

            @pl.when(jnp.logical_and(q > 0, lax.rem(step, blocks) == 0))
            def _():
                row_copy(q).wait_recv()

        s = flip(lax.div(c, cols_each), k, n_col // cols_each) * blocks + lax.rem(step, blocks)
        wanted = jnp.concatenate(
            [
                jnp.maximum(idx_all[group * s + i], idx_all[group * s + i + 1])
                for i in range(0, group, 2)
            ],
            axis=1,
        )
        which = jnp.right_shift(wanted, chunk.bit_length() - 1)
        offset = jnp.bitwise_and(wanted, chunk - 1).astype(F32).astype(BF16)
        picks = jnp.where(small == offset, jnp.ones_like(small), jnp.zeros_like(small))

        if chunks <= 8:
            taken = dot(coarse_split[...], picks)
            acc = jnp.zeros((2 * part, span), F32)
            for k in range(chunks):
                acc = jnp.where(which == k, taken[2 * part * k : 2 * part * (k + 1)], acc)
        else:

            def one_chunk(k, acc):
                rows = pl.ds(pl.multiple_of(2 * part * k, 2 * part), 2 * part)
                return jnp.where(which == k, dot(coarse_split[rows, :], picks), acc)

            acc = lax.fori_loop(0, chunks, one_chunk, jnp.zeros((2 * part, span), F32))
        values = join(acc)
        top = values.astype(BF16)
        at = pl.ds(pl.multiple_of(s * span, span), span)
        columns[:part, at] = top
        columns[half : half + part, at] = (values - top.astype(F32)).astype(BF16)
        return carry

    lax.fori_loop(0, count // group, one_column, 0)

    def gathered(buffer):
        return split(
            jnp.concatenate([unpack(buffer[s], buffer[s + 1]) for s in range(0, count, 2)], axis=1)
        )

    arrive(val_all.at[0], RHS)
    solved = join(dot_nt(gathered(val_all.at[0]), columns[...]))
    solved = solved + pltpu.roll(solved, half, 1)
    val_all[1, me] = pack(solved)
    start(val_all.at[1], SOL)

    pl.when(c < n_col // 4)(last_sweep)

    for slot in range(4):
        @pl.when(flags[slot])
        def _():
            near_copy(slot).wait_recv()

        @pl.when(jnp.logical_not(flags[slot]))
        def _():
            near_in[slot] = jnp.full(near_in.shape[1:], -1, jnp.int32)

    def inverse(order_hot):
        order = lax.broadcasted_iota(jnp.int32, (8, face), 1).astype(F32)
        return join(dot_nt(split(order), order_hot[...]))[:1]

    def in_turn(rows):
        joined = None
        for i, row in enumerate(rows):
            wide_place[...] = jnp.full(wide_place.shape, -1, jnp.int32)
            wide_place[:1, :lanes] = row
            row = wide_place[...]
            row = pltpu.roll(row, i * nprim, 1) if i else row
            joined = row if joined is None else jnp.maximum(joined, row)
        return joined[:1]

    west, east, south, north = [near_in[slot] for slot in range(4)]
    target = in_turn(
        [
            numbers,
            look_up(inverse(west_hot), west[1:2] - face, 0),
            east[2:3],
            look_up(inverse(south_hot), south[1:2] - 3 * face, 2 * face),
            north[3:4],
        ]
    )
    wanted_coarse = in_turn([near_out[:1, :]] + [near[:1] for near in (west, east, south, north)])
    target = jnp.broadcast_to(target.astype(F32), (8, five)).T[:, :1].astype(jnp.int32)
    place_hot[...] = jnp.where(
        lax.broadcasted_iota(jnp.int32, (five, unknowns), 1) == target, weights, 0.0
    ).astype(BF16)
    spread = dot(place_hot[...], schur_hi[...]) + dot(place_hot[...], schur_lo[...])
    top = spread.astype(BF16)
    spread_hi[...] = top
    spread_lo[...] = (spread - top.astype(F32)).astype(BF16)

    at = lax.broadcasted_iota(jnp.int32, (wide, five), 0)
    upper = (at >= half).astype(jnp.int32)
    number = upper * coarse_rows + at - upper * half
    number = jnp.where(at - upper * half < coarse_rows, number, -2 * coarse_all)

    def one_pick(s, carry):
        coarse_hot[pl.ds(pl.multiple_of(s * wide, wide), wide), :] = one_hot(
            number, wanted_coarse - s * 2 * coarse_rows
        )
        return carry

    lax.fori_loop(0, count // 2, one_pick, 0)
    before = face_finish(1, weights * local[...])
    image_before = apply(schur_hi, schur_lo, before)

    def lane_sum(values):
        return jnp.sum(values, axis=1, keepdims=True)

    arrive(val_all.at[1], SOL)
    read = split(join(dot(gathered(val_all.at[1]), coarse_hot[...])))
    precond = before + join(dot(read, place_hot[...]))
    image = image_before + join(dot(read, spread_hi[...]) + dot(read, spread_lo[...]))
    rz = lane_sum(scaled * precond)
    pq = lane_sum(precond * image)
    sum_lane = lax.broadcasted_iota(jnp.int32, (rhs, 128), 1)
    sum_case = lax.broadcasted_iota(jnp.int32, (rhs, 128), 0)
    upper_lane, lower_lane = sum_lane == sum_case + rhs, sum_lane == sum_case
    laid = jnp.where(lower_lane, rz, 0.0) + jnp.where(upper_lane, pq, 0.0)
    sum_all[me] = jnp.sum(laid, axis=0, keepdims=True)
    start(sum_all, SUM)
    face_fill(2, image)
    when_neighbour(can_send, lambda slot: face_copy(2, slot).start())
    direction[...] = precond
    loads_out[...] = right_side
    await_some(idx_all, n_row - 1, idx_send.at[0])
    await_some(idx_all, n_row * (n_col - 1), idx_send.at[1])
    await_all(val_all.at[0], all_send.at[RHS])
    await_all(val_all.at[1], all_send.at[SOL])
    for turn in range(2):
        when_neighbour(can_send, lambda slot: face_copy(turn, slot).wait_send())
    when_neighbour(can_send, lambda slot: near_copy(slot).wait_send())
    image_out[...] = face_finish(2, image)
    arrive(sum_all, SUM)
    parts = [sum_all[i] for i in range(count)]
    while len(parts) > 1:
        parts = [x + y for x, y in zip(parts[::2], parts[1::2])]
    sums = jnp.broadcast_to(parts[0], (rhs, 128))
    alpha = lane_sum(jnp.where(lower_lane, sums, 0.0)) / lane_sum(jnp.where(upper_lane, sums, 0.0))
    alpha_out[...] = jnp.broadcast_to(alpha, alpha_out.shape)
    await_all(sum_all, all_send.at[SUM])
    when_neighbour(can_send, lambda slot: face_copy(2, slot).wait_send())


def up(n, to):
    return -(-n // to) * to


def body(
    n_row, n_col, loads, schur, factor, coarse_inverse, elements, west_map, south_map,
    prim_local, prim_coarse,
):
    vectors = loads[0, 0].T
    rhs, unknowns = vectors.shape
    face = unknowns // 4
    coarse_rows, coarse_all = coarse_inverse.shape
    nprim = prim_local.shape[2]
    wide = 2 * up(max(nprim, coarse_rows), 64)
    count = n_row * n_col
    lanes, five = up(nprim, 128), up(5 * nprim, 128)
    vmem = pl.BlockSpec(memory_space=pltpu.VMEM)
    hbm = pl.BlockSpec(memory_space=pl.ANY)
    dma = pltpu.SemaphoreType.DMA
    out = pltpu.VMEM(vectors.shape, F32)
    direction, image, right_side, alpha = pl.pallas_call(
        functools.partial(kernel, n_row, n_col),
        out_shape=(out, out, out, out),
        in_specs=[hbm] * 9,
        out_specs=(vmem, vmem, vmem, vmem),
        scratch_shapes=[
            pltpu.VMEM(vectors.shape, F32),
            pltpu.VMEM((1, 1), jnp.int32),
            pltpu.VMEM((1, face), jnp.int32),
            pltpu.VMEM((1, face), jnp.int32),
            pltpu.VMEM((1, nprim), jnp.int32),
            pltpu.VMEM((1, nprim), jnp.int32),
            pltpu.VMEM((unknowns, unknowns), F32),
            pltpu.VMEM((unknowns, unknowns), F32),
            pltpu.VMEM((coarse_rows, coarse_all), F32),
            pltpu.VMEM((unknowns, unknowns), BF16),
            pltpu.VMEM((unknowns, unknowns), BF16),
            pltpu.VMEM((unknowns, unknowns), BF16),
            pltpu.VMEM((unknowns, unknowns), BF16),
            pltpu.VMEM((coarse_all // face * 2 * up(coarse_rows, 16), face), BF16),
            pltpu.VMEM((wide, count // 2 * wide), BF16),
            pltpu.VMEM((face, face), BF16),
            pltpu.VMEM((face, face), BF16),
            pltpu.VMEM((unknowns, wide), BF16),
            pltpu.VMEM((count // 2 * wide, five), BF16),
            pltpu.VMEM((five, unknowns), BF16),
            pltpu.VMEM((five, unknowns), BF16),
            pltpu.VMEM((five, unknowns), BF16),
            pltpu.VMEM(vectors.shape, F32),
            pltpu.VMEM((8, wide), jnp.int32),
            pltpu.VMEM((8, five), jnp.int32),
            pltpu.VMEM((count, 1, wide), jnp.int32),
            pltpu.VMEM((2, count, rhs // 2, wide), F32),
            pltpu.VMEM((count, 1, 128), F32),
            pltpu.VMEM((3, 4, rhs, face), F32),
            pltpu.VMEM((3, 4, rhs, face), F32),
            pltpu.VMEM((4, lanes), jnp.int32),
            pltpu.VMEM((4, 4, lanes), jnp.int32),
            dma((9,)),
            dma((3, 4)),
            dma((3, 4)),
            dma((4,)),
            dma((4,)),
            dma((2,)),
            dma((n_col,)),
            dma((3,)),
            dma((3,)),
            pltpu.SemaphoreType.REGULAR,
        ],
        compiler_params=pltpu.CompilerParams(collective_id=0, has_side_effects=True),
    )(
        vectors, schur[0, 0], factor[0, 0], coarse_inverse, elements,
        west_map[0], south_map[0], prim_local[0], prim_coarse[0],
    )
    solution = alpha * direction
    residual = right_side - alpha * image
    return solution.T[None, None], residual.T[None, None]


def solution(mesh):
    placed = (
        P("row", "col", None, None),
        P("row", "col", None, None),
        P("row", "col", None, None),
        P(("row", "col"), None),
        P("row", "col"),
        P("row", "col", None),
        P("row", "col", None),
        P("row", "col", None),
        P("row", "col", None),
    )
    return jax.shard_map(
        functools.partial(body, mesh.shape["row"], mesh.shape["col"]),
        mesh=mesh,
        in_specs=placed,
        out_specs=(P("row", "col", None, None), P("row", "col", None, None)),
        check_vma=False,
    )
```

```python
import functools

import jax
import jax.numpy as jnp
from jax import lax
from jax.experimental import pallas as pl
from jax.experimental.pallas import tpu as pltpu
from jax.sharding import PartitionSpec as P

ELEM_BASE = 4096
MOST_SWEEPS = 3
MESH = pl.DeviceIdType.MESH
F32, BF16 = jnp.float32, jnp.bfloat16
NT = (((1,), (1,)), ((), ()))
RHS, SOL, SUM = range(3)


def split(values):
    high = values.astype(BF16).astype(F32)
    return jnp.concatenate([high, values - high], axis=0).astype(BF16)


def join(stacked):
    rows = stacked.shape[0] // 2
    return stacked[:rows] + stacked[rows:]


def one_hot(numbers, wanted):
    return jnp.where(numbers == wanted, 1.0, 0.0).astype(BF16)


def dot(a, b):
    return jnp.dot(a, b, preferred_element_type=F32)


def dot_nt(a, b):
    return lax.dot_general(a, b, NT, preferred_element_type=F32)


def flip(value, mask, size):
    out, weight = 0, 1
    while weight < size:
        bit = lax.rem(lax.div(value, weight), 2)
        if isinstance(mask, int):
            bit = 1 - bit if (mask // weight) % 2 else bit
        else:
            bit = lax.rem(bit + lax.rem(lax.div(mask, weight), 2), 2)
        out, weight = out + weight * bit, 2 * weight
    return out


def kernel(
    n_row, n_col, loads_hbm, schur_hbm, factor_hbm, coarse_hbm, elements_hbm, west_hbm, south_hbm,
    local_hbm, prim_hbm, direction, image_out, loads_out, alpha_out,
    loads, elements, west_map, south_map, prim_local, prim_coarse,
    schur_in, factor_in, coarse_in, schur_hi, schur_lo, factor_hi, factor_lo,
    coarse_split, columns, west_hot, south_hot, local_hot, coarse_hot, place_hot, spread_hi, spread_lo, local,
    place, wide_place, idx_all, val_all, sum_all, face_out, face_in, near_out, near_in,
    copy_sem, face_send, face_recv, near_send, near_recv, idx_send, idx_recv, all_send, all_recv, entered,
):
    a, c = lax.axis_index("row"), lax.axis_index("col")
    unknowns = loads.shape[1]
    face = unknowns // 4
    wide = local_hot.shape[1]
    half = wide // 2
    count = n_row * n_col
    me = a * n_col + c
    spot = c * n_row + a
    odd = lax.rem(a, 2)
    coarse_rows, coarse_all = coarse_in.shape
    nprim = prim_local.shape[1]
    lanes = near_out.shape[1]
    five = place_hot.shape[0]

    copies = [
        pltpu.make_async_copy(src, dst, copy_sem.at[i])
        for i, (src, dst) in enumerate(
            [
                (factor_hbm, factor_in), (coarse_hbm, coarse_in), (schur_hbm, schur_in),
                (loads_hbm, loads), (west_hbm, west_map), (south_hbm, south_map),
                (local_hbm, prim_local), (prim_hbm, prim_coarse), (elements_hbm, elements),
            ]
        )
    ]
    barrier = pltpu.get_barrier_semaphore()
    column_mates = [(flip(a, m, n_row), c) for m in range(1, n_row)]
    row_mates = [(a, flip(c, m, n_col)) for m in range(1, n_col)]
    for mate in row_mates + column_mates:
        pl.semaphore_signal(barrier, inc=1, device_id=mate, device_id_type=MESH)
    for copy in copies[3:] + copies[:3]:
        copy.start()

    rows_of = [flip(a, m, n_row) for m in range(n_row)]
    cols_of = [flip(c, m, n_col) for m in range(n_col)]

    def peer(m):
        if not isinstance(m, int):
            return (flip(a, lax.div(m, n_col), n_row), flip(c, lax.rem(m, n_col), n_col))
        return (rows_of[m // n_col], cols_of[m % n_col])

    def each(work):
        if count <= 64:
            for m in range(count - 1, 0, -1):
                work(m)
        else:
            lax.fori_loop(1, count, lambda d, carry: (work(count - d), carry)[1], 0)

    for copy in copies[3:]:
        copy.wait()

    def hot(order_ref):
        return one_hot(lax.broadcasted_iota(jnp.int32, (face, face), 0), order_ref[...])

    west_hot[...] = hot(west_map)
    south_hot[...] = hot(south_map)

    lane = lax.broadcasted_iota(jnp.int32, (1, unknowns), 1)
    flags = [c > 0, c < n_col - 1, a > 0, a < n_row - 1]
    halves = [jnp.where(flag, 0.5, 1.0).astype(F32) for flag in flags]
    weights = jnp.where(
        lane < face,
        halves[0],
        jnp.where(lane < 2 * face, halves[1], jnp.where(lane < 3 * face, halves[2], halves[3])),
    )
    targets = [(a, c + 1), (a, c - 1), (a + 1, c), (a - 1, c)]
    can_send = [flags[1], flags[0], flags[3], flags[2]]

    def face_copy(turn, slot):
        return pltpu.make_async_remote_copy(
            src_ref=face_out.at[turn, slot],
            dst_ref=face_in.at[turn, slot],
            send_sem=face_send.at[turn, slot],
            recv_sem=face_recv.at[turn, slot],
            device_id=targets[slot],
            device_id_type=MESH,
        )

    def near_copy(slot):
        return pltpu.make_async_remote_copy(
            src_ref=near_out,
            dst_ref=near_in.at[slot],
            send_sem=near_send.at[slot],
            recv_sem=near_recv.at[slot],
            device_id=targets[slot],
            device_id_type=MESH,
        )

    def face_fill(turn, values):
        face_out[turn, 0] = values[:, face : 2 * face]
        face_out[turn, 2] = values[:, 3 * face :]
        face_out[turn, 1] = join(dot_nt(split(values[:, :face]), west_hot[...]))
        face_out[turn, 3] = join(dot_nt(split(values[:, 2 * face : 3 * face]), south_hot[...]))

    def when_neighbour(present, work):
        for slot in range(4):
            @pl.when(present[slot])
            def _():
                work(slot)

    def face_finish(turn, values):
        for slot in range(4):
            @pl.when(flags[slot])
            def _():
                face_copy(turn, slot).wait_recv()

            @pl.when(jnp.logical_not(flags[slot]))
            def _():
                face_in[turn, slot] = jnp.zeros(face_in.shape[2:], F32)
        adds = [
            join(dot(split(face_in[turn, 0]), west_hot[...])),
            face_in[turn, 1],
            join(dot(split(face_in[turn, 2]), south_hot[...])),
            face_in[turn, 3],
        ]
        return values + jnp.concatenate(adds, axis=1)

    def column_copy(m):
        return pltpu.make_async_remote_copy(
            src_ref=idx_all.at[spot],
            dst_ref=idx_all.at[spot],
            send_sem=idx_send.at[0],
            recv_sem=idx_recv.at[0],
            device_id=column_mates[m - 1],
            device_id_type=MESH,
        )

    def row_copy(m):
        own = idx_all.at[pl.ds(c * n_row, n_row)]
        return pltpu.make_async_remote_copy(
            src_ref=own,
            dst_ref=own,
            send_sem=idx_send.at[1],
            recv_sem=idx_recv.at[m],
            device_id=(a, cols_of[m] if isinstance(m, int) else flip(c, m, n_col)),
            device_id_type=MESH,
        )

    first = loads[...]
    face_fill(0, first)
    pl.semaphore_wait(barrier, n_row + n_col - 2)
    for mate in column_mates:
        pl.semaphore_signal(entered, inc=1, device_id=mate, device_id_type=MESH)
    when_neighbour(can_send, lambda slot: face_copy(0, slot).start())

    def placed(source):
        place[...] = jnp.full(place.shape, -1, jnp.int32)
        place[:1, :nprim] = source[...]
        base = place[...]
        return base, pltpu.roll(base, half, 1)

    base, rolled = placed(prim_coarse)
    own_coarse = jnp.where(odd == 1, rolled, base)[:1]
    idx_all[spot] = own_coarse
    for m in range(1, n_row):
        column_copy(m).start()
    own_base, own_rolled = placed(prim_local)
    own_ids, numbers = base[:1], own_base[:1]
    depth = lax.broadcasted_iota(jnp.int32, (face, lanes), 0)

    def look_up(table, numbers, offset):
        inside = jnp.logical_and(numbers >= 0, numbers < face)
        table = jnp.broadcast_to(table, (8, face)).astype(F32)
        found = join(dot(split(table), one_hot(depth, numbers)))[:1]
        return jnp.where(inside, found.astype(jnp.int32) + offset, -1)

    to_west = look_up(west_map[...], numbers, face)
    to_south = look_up(south_map[...], numbers - 2 * face, 3 * face)
    row = lax.broadcasted_iota(jnp.int32, near_out.shape, 0)
    near_out[...] = jnp.where(
        row == 0, own_ids, jnp.where(row == 1, numbers, jnp.where(row == 2, to_west, to_south))
    )
    when_neighbour(can_send, lambda slot: near_copy(slot).start())

    own_local = jnp.maximum(own_base, own_rolled)[:1]
    rows_iota = lax.broadcasted_iota(jnp.int32, (unknowns, wide), 0)
    local_hot[...] = one_hot(rows_iota, own_local)

    def all_copy(buffer, kind, m):
        return pltpu.make_async_remote_copy(
            src_ref=buffer.at[spot if kind == RHS else me],
            dst_ref=buffer.at[spot if kind == RHS else me],
            send_sem=all_send.at[kind],
            recv_sem=all_recv.at[kind],
            device_id=peer(m),
            device_id_type=MESH,
        )

    def start(buffer, kind):
        each(lambda m: all_copy(buffer, kind, m).start())

    def await_some(buffer, sent, semaphore):
        slots = buffer.at[pl.ds(0, sent)]
        pltpu.make_async_copy(slots, slots, semaphore).wait()

    def await_all(buffer, semaphore):
        await_some(buffer, count - 1, semaphore)

    def arrive(buffer, kind):
        await_all(buffer, all_recv.at[kind])

    rhs = loads.shape[0]
    lower = lax.broadcasted_iota(jnp.int32, (rhs // 2, wide), 1) < half

    def pack(values):
        return jnp.where(lower, values[: rhs // 2], values[rhs // 2 :])

    square = (rhs, wide)
    stays = (lax.broadcasted_iota(jnp.int32, square, 1) < half) == (
        lax.broadcasted_iota(jnp.int32, square, 0) < rhs // 2
    )

    def unpack(first, second):
        both = jnp.concatenate([first, second], axis=0)
        return jnp.where(stays, both, pltpu.roll(pltpu.roll(both, half, 1), rhs // 2, 0))

    def split_matrix(source, high, low):
        step = 128

        def one(i, carry):
            at = pl.ds(pl.multiple_of(i * step, step), step)
            values = source[at, :]
            top = values.astype(BF16)
            high[at, :] = top
            low[at, :] = (values - top.astype(F32)).astype(BF16)
            return carry

        lax.fori_loop(0, source.shape[0] // step, one, 0)

    chunk = coarse_split.shape[1]
    chunks = coarse_all // chunk
    part = coarse_split.shape[0] // chunks // 2

    def over_chunks(work, carry):
        if chunks <= 8:
            for k in range(chunks):
                carry = work(k, carry)
            return carry
        return lax.fori_loop(0, chunks, work, carry)

    def split_coarse():
        copies[1].wait()
        columns[...] = jnp.zeros(columns.shape, BF16)
        if coarse_rows < part:
            coarse_split[...] = jnp.zeros(coarse_split.shape, BF16)

        def one(k, carry):
            at = k * chunk if isinstance(k, int) else pl.multiple_of(k * chunk, chunk)
            rows = 2 * part * k if isinstance(k, int) else pl.multiple_of(2 * part * k, 2 * part)
            values = coarse_in[:, pl.ds(at, chunk)]
            top = values.astype(BF16)
            coarse_split[pl.ds(rows, coarse_rows), :] = top
            coarse_split[pl.ds(rows + part, coarse_rows), :] = (values - top.astype(F32)).astype(BF16)
            return carry

        over_chunks(one, 0)

    early = c < n_col // 2

    def split_schur():
        copies[2].wait()
        split_matrix(schur_in, schur_hi, schur_lo)

    copies[0].wait()
    split_matrix(factor_in, factor_hi, factor_lo)
    split_coarse()
    pl.when(early)(split_schur)
    right_side = face_finish(0, first)
    scaled = weights * right_side
    val_all[0, spot] = pack(join(dot(split(scaled), local_hot[...])))
    await_some(idx_all, n_row - 1, idx_recv.at[0])
    pl.semaphore_wait(entered, n_row - 1)
    start(val_all.at[0], RHS)
    for m in range(1, n_col):
        row_copy(m).start()

    def apply(high, low, vectors):
        both = split(vectors)
        return join(dot(both, high[...]) + dot(both, low[...]))

    pl.when(jnp.logical_not(early))(split_schur)
    local[...] = apply(factor_hi, factor_lo, scaled)

    def sweep(turn):
        now = local[...]
        inner = scaled - apply(schur_hi, schur_lo, now)
        later = now + apply(factor_hi, factor_lo, inner)
        more = jnp.broadcast_to(elements[...], now.shape) >= turn * ELEM_BASE
        local[...] = jnp.where(more, later, now)

    def last_sweep():
        sweep(MOST_SWEEPS)
        face_fill(1, weights * local[...])
        when_neighbour(can_send, lambda slot: face_copy(1, slot).start())

    for turn in range(2, MOST_SWEEPS):
        sweep(turn)
    pl.when(c >= n_col // 4)(last_sweep)

    group = 8
    span = group // 2 * wide
    small = lax.broadcasted_iota(jnp.int32, (chunk, span), 0).astype(F32).astype(BF16)
    cols_each, blocks = max(1, group // n_row), max(1, n_row // group)

    def one_column(step, carry):
        k = lax.div(step, blocks)
        for i in range(cols_each):
            q = k * cols_each + i

            @pl.when(jnp.logical_and(q > 0, lax.rem(step, blocks) == 0))
            def _():
                row_copy(q).wait_recv()

        s = flip(lax.div(c, cols_each), k, n_col // cols_each) * blocks + lax.rem(step, blocks)
        wanted = jnp.concatenate(
            [
                jnp.maximum(idx_all[group * s + i], idx_all[group * s + i + 1])
                for i in range(0, group, 2)
            ],
            axis=1,
        )
        which = jnp.right_shift(wanted, chunk.bit_length() - 1)
        offset = jnp.bitwise_and(wanted, chunk - 1).astype(F32).astype(BF16)
        picks = jnp.where(small == offset, jnp.ones_like(small), jnp.zeros_like(small))

        if chunks <= 8:
            taken = dot(coarse_split[...], picks)
            acc = jnp.zeros((2 * part, span), F32)
            for k in range(chunks):
                acc = jnp.where(which == k, taken[2 * part * k : 2 * part * (k + 1)], acc)
        else:

            def one_chunk(k, acc):
                rows = pl.ds(pl.multiple_of(2 * part * k, 2 * part), 2 * part)
                return jnp.where(which == k, dot(coarse_split[rows, :], picks), acc)

            acc = lax.fori_loop(0, chunks, one_chunk, jnp.zeros((2 * part, span), F32))
        values = join(acc)
        top = values.astype(BF16)
        at = pl.ds(pl.multiple_of(s * span, span), span)
        columns[:part, at] = top
        columns[half : half + part, at] = (values - top.astype(F32)).astype(BF16)
        return carry

    lax.fori_loop(0, count // group, one_column, 0)

    def gathered(buffer):
        return split(
            jnp.concatenate([unpack(buffer[s], buffer[s + 1]) for s in range(0, count, 2)], axis=1)
        )

    arrive(val_all.at[0], RHS)
    solved = join(dot_nt(gathered(val_all.at[0]), columns[...]))
    solved = solved + pltpu.roll(solved, half, 1)
    val_all[1, me] = pack(solved)
    start(val_all.at[1], SOL)

    pl.when(c < n_col // 4)(last_sweep)

    for slot in range(4):
        @pl.when(flags[slot])
        def _():
            near_copy(slot).wait_recv()

        @pl.when(jnp.logical_not(flags[slot]))
        def _():
            near_in[slot] = jnp.full(near_in.shape[1:], -1, jnp.int32)

    def inverse(order_hot):
        order = lax.broadcasted_iota(jnp.int32, (8, face), 1).astype(F32)
        return join(dot_nt(split(order), order_hot[...]))[:1]

    def in_turn(rows):
        joined = None
        for i, row in enumerate(rows):
            wide_place[...] = jnp.full(wide_place.shape, -1, jnp.int32)
            wide_place[:1, :lanes] = row
            row = wide_place[...]
            row = pltpu.roll(row, i * nprim, 1) if i else row
            joined = row if joined is None else jnp.maximum(joined, row)
        return joined[:1]

    west, east, south, north = [near_in[slot] for slot in range(4)]
    target = in_turn(
        [
            numbers,
            look_up(inverse(west_hot), west[1:2] - face, 0),
            east[2:3],
            look_up(inverse(south_hot), south[1:2] - 3 * face, 2 * face),
            north[3:4],
        ]
    )
    wanted_coarse = in_turn([own_ids] + [near[:1] for near in (west, east, south, north)])
    target = jnp.broadcast_to(target.astype(F32), (8, five)).T[:, :1].astype(jnp.int32)
    place_hot[...] = jnp.where(
        lax.broadcasted_iota(jnp.int32, (five, unknowns), 1) == target, weights, 0.0
    ).astype(BF16)
    spread = dot(place_hot[...], schur_hi[...]) + dot(place_hot[...], schur_lo[...])
    top = spread.astype(BF16)
    spread_hi[...] = top
    spread_lo[...] = (spread - top.astype(F32)).astype(BF16)

    at = lax.broadcasted_iota(jnp.int32, (wide, five), 0)
    upper = (at >= half).astype(jnp.int32)
    number = upper * coarse_rows + at - upper * half
    number = jnp.where(at - upper * half < coarse_rows, number, -2 * coarse_all)

    def one_pick(s, carry):
        coarse_hot[pl.ds(pl.multiple_of(s * wide, wide), wide), :] = one_hot(
            number, wanted_coarse - s * 2 * coarse_rows
        )
        return carry

    lax.fori_loop(0, count // 2, one_pick, 0)
    before = face_finish(1, weights * local[...])
    image_before = apply(schur_hi, schur_lo, before)

    def lane_sum(values):
        return jnp.sum(values, axis=1, keepdims=True)

    arrive(val_all.at[1], SOL)
    read = split(join(dot(gathered(val_all.at[1]), coarse_hot[...])))
    precond = before + join(dot(read, place_hot[...]))
    image = image_before + join(dot(read, spread_hi[...]) + dot(read, spread_lo[...]))
    rz = lane_sum(scaled * precond)
    pq = lane_sum(precond * image)
    sum_lane = lax.broadcasted_iota(jnp.int32, (rhs, 128), 1)
    sum_case = lax.broadcasted_iota(jnp.int32, (rhs, 128), 0)
    upper_lane, lower_lane = sum_lane == sum_case + rhs, sum_lane == sum_case
    laid = jnp.where(lower_lane, rz, 0.0) + jnp.where(upper_lane, pq, 0.0)
    sum_all[me] = jnp.sum(laid, axis=0, keepdims=True)
    start(sum_all, SUM)
    face_fill(2, image)
    when_neighbour(can_send, lambda slot: face_copy(2, slot).start())
    direction[...] = precond
    loads_out[...] = right_side
    await_some(idx_all, n_row - 1, idx_send.at[0])
    await_some(idx_all, n_row * (n_col - 1), idx_send.at[1])
    await_all(val_all.at[0], all_send.at[RHS])
    await_all(val_all.at[1], all_send.at[SOL])
    for turn in range(2):
        when_neighbour(can_send, lambda slot: face_copy(turn, slot).wait_send())
    when_neighbour(can_send, lambda slot: near_copy(slot).wait_send())
    image_out[...] = face_finish(2, image)
    arrive(sum_all, SUM)
    parts = [sum_all[i] for i in range(count)]
    while len(parts) > 1:
        parts = [x + y for x, y in zip(parts[::2], parts[1::2])]
    sums = jnp.broadcast_to(parts[0], (rhs, 128))
    alpha = lane_sum(jnp.where(lower_lane, sums, 0.0)) / lane_sum(jnp.where(upper_lane, sums, 0.0))
    alpha_out[...] = jnp.broadcast_to(alpha, alpha_out.shape)
    await_all(sum_all, all_send.at[SUM])
    when_neighbour(can_send, lambda slot: face_copy(2, slot).wait_send())


def up(n, to):
    return -(-n // to) * to


def body(
    n_row, n_col, loads, schur, factor, coarse_inverse, elements, west_map, south_map,
    prim_local, prim_coarse,
):
    vectors = loads[0, 0].T
    rhs, unknowns = vectors.shape
    face = unknowns // 4
    coarse_rows, coarse_all = coarse_inverse.shape
    nprim = prim_local.shape[2]
    wide = 2 * up(max(nprim, coarse_rows), 64)
    count = n_row * n_col
    lanes, five = wide, max(wide, up(5 * nprim, 128))
    vmem = pl.BlockSpec(memory_space=pltpu.VMEM)
    hbm = pl.BlockSpec(memory_space=pl.ANY)
    dma = pltpu.SemaphoreType.DMA
    out = pltpu.VMEM(vectors.shape, F32)
    direction, image, right_side, alpha = pl.pallas_call(
        functools.partial(kernel, n_row, n_col),
        out_shape=(out, out, out, out),
        in_specs=[hbm] * 9,
        out_specs=(vmem, vmem, vmem, vmem),
        scratch_shapes=[
            pltpu.VMEM(vectors.shape, F32),
            pltpu.VMEM((1, 1), jnp.int32),
            pltpu.VMEM((1, face), jnp.int32),
            pltpu.VMEM((1, face), jnp.int32),
            pltpu.VMEM((1, nprim), jnp.int32),
            pltpu.VMEM((1, nprim), jnp.int32),
            pltpu.VMEM((unknowns, unknowns), F32),
            pltpu.VMEM((unknowns, unknowns), F32),
            pltpu.VMEM((coarse_rows, coarse_all), F32),
            pltpu.VMEM((unknowns, unknowns), BF16),
            pltpu.VMEM((unknowns, unknowns), BF16),
            pltpu.VMEM((unknowns, unknowns), BF16),
            pltpu.VMEM((unknowns, unknowns), BF16),
            pltpu.VMEM((coarse_all // face * 2 * up(coarse_rows, 16), face), BF16),
            pltpu.VMEM((wide, count // 2 * wide), BF16),
            pltpu.VMEM((face, face), BF16),
            pltpu.VMEM((face, face), BF16),
            pltpu.VMEM((unknowns, wide), BF16),
            pltpu.VMEM((count // 2 * wide, five), BF16),
            pltpu.VMEM((five, unknowns), BF16),
            pltpu.VMEM((five, unknowns), BF16),
            pltpu.VMEM((five, unknowns), BF16),
            pltpu.VMEM(vectors.shape, F32),
            pltpu.VMEM((8, wide), jnp.int32),
            pltpu.VMEM((8, five), jnp.int32),
            pltpu.VMEM((count, 1, wide), jnp.int32),
            pltpu.VMEM((2, count, rhs // 2, wide), F32),
            pltpu.VMEM((count, 1, 128), F32),
            pltpu.VMEM((3, 4, rhs, face), F32),
            pltpu.VMEM((3, 4, rhs, face), F32),
            pltpu.VMEM((8, lanes), jnp.int32),
            pltpu.VMEM((4, 8, lanes), jnp.int32),
            dma((9,)),
            dma((3, 4)),
            dma((3, 4)),
            dma((4,)),
            dma((4,)),
            dma((2,)),
            dma((n_col,)),
            dma((3,)),
            dma((3,)),
            pltpu.SemaphoreType.REGULAR,
        ],
        compiler_params=pltpu.CompilerParams(collective_id=0, has_side_effects=True),
    )(
        vectors, schur[0, 0], factor[0, 0], coarse_inverse, elements,
        west_map[0], south_map[0], prim_local[0], prim_coarse[0],
    )
    solution = alpha * direction
    residual = right_side - alpha * image
    return solution.T[None, None], residual.T[None, None]


def solution(mesh):
    placed = (
        P("row", "col", None, None),
        P("row", "col", None, None),
        P("row", "col", None, None),
        P(("row", "col"), None),
        P("row", "col"),
        P("row", "col", None),
        P("row", "col", None),
        P("row", "col", None),
        P("row", "col", None),
    )
    return jax.shard_map(
        functools.partial(body, mesh.shape["row"], mesh.shape["col"]),
        mesh=mesh,
        in_specs=placed,
        out_specs=(P("row", "col", None, None), P("row", "col", None, None)),
        check_vma=False,
    )
```

```python
import functools

import jax
import jax.numpy as jnp
from jax import lax
from jax.experimental import pallas as pl
from jax.experimental.pallas import tpu as pltpu
from jax.sharding import PartitionSpec as P

ELEM_BASE = 4096
MOST_SWEEPS = 3
MESH = pl.DeviceIdType.MESH
F32, BF16 = jnp.float32, jnp.bfloat16
NT = (((1,), (1,)), ((), ()))
RHS, SOL, SUM = range(3)


def split(values):
    high = values.astype(BF16).astype(F32)
    return jnp.concatenate([high, values - high], axis=0).astype(BF16)


def join(stacked):
    rows = stacked.shape[0] // 2
    return stacked[:rows] + stacked[rows:]


def one_hot(numbers, wanted):
    return jnp.where(numbers == wanted, 1.0, 0.0).astype(BF16)


def dot(a, b):
    return jnp.dot(a, b, preferred_element_type=F32)


def dot_nt(a, b):
    return lax.dot_general(a, b, NT, preferred_element_type=F32)


def flip(value, mask, size):
    out, weight = 0, 1
    while weight < size:
        bit = lax.rem(lax.div(value, weight), 2)
        if isinstance(mask, int):
            bit = 1 - bit if (mask // weight) % 2 else bit
        else:
            bit = lax.rem(bit + lax.rem(lax.div(mask, weight), 2), 2)
        out, weight = out + weight * bit, 2 * weight
    return out


def kernel(
    n_row, n_col, loads_hbm, schur_hbm, factor_hbm, coarse_hbm, elements_hbm, west_hbm, south_hbm,
    local_hbm, prim_hbm, direction, image_out, loads_out, alpha_out,
    loads, elements, west_map, south_map, prim_local, prim_coarse,
    schur_in, factor_in, coarse_in, schur_hi, schur_lo, factor_hi, factor_lo,
    coarse_split, columns, west_hot, south_hot, local_hot, coarse_hot, place_hot, spread_hi, spread_lo, local,
    place, wide_place, idx_all, val_all, sum_all, face_out, face_in, near_out, near_in,
    copy_sem, face_send, face_recv, near_send, near_recv, idx_send, idx_recv, all_send, all_recv, entered,
):
    a, c = lax.axis_index("row"), lax.axis_index("col")
    unknowns = loads.shape[1]
    face = unknowns // 4
    wide = local_hot.shape[1]
    half = wide // 2
    count = n_row * n_col
    me = a * n_col + c
    spot = c * n_row + a
    odd = lax.rem(a, 2)
    coarse_rows, coarse_all = coarse_in.shape
    nprim = prim_local.shape[1]
    lanes = near_out.shape[1]
    five = place_hot.shape[0]

    copies = [
        pltpu.make_async_copy(src, dst, copy_sem.at[i])
        for i, (src, dst) in enumerate(
            [
                (factor_hbm, factor_in), (coarse_hbm, coarse_in), (schur_hbm, schur_in),
                (loads_hbm, loads), (west_hbm, west_map), (south_hbm, south_map),
                (local_hbm, prim_local), (prim_hbm, prim_coarse), (elements_hbm, elements),
            ]
        )
    ]
    barrier = pltpu.get_barrier_semaphore()
    column_mates = [(flip(a, m, n_row), c) for m in range(1, n_row)]
    row_mates = [(a, flip(c, m, n_col)) for m in range(1, n_col)]
    for mate in row_mates + column_mates:
        pl.semaphore_signal(barrier, inc=1, device_id=mate, device_id_type=MESH)
    for copy in copies[3:] + copies[:3]:
        copy.start()

    rows_of = [flip(a, m, n_row) for m in range(n_row)]
    cols_of = [flip(c, m, n_col) for m in range(n_col)]

    def peer(m):
        if not isinstance(m, int):
            return (flip(a, lax.div(m, n_col), n_row), flip(c, lax.rem(m, n_col), n_col))
        return (rows_of[m // n_col], cols_of[m % n_col])

    def each(work):
        if count <= 64:
            for m in range(count - 1, 0, -1):
                work(m)
        else:
            lax.fori_loop(1, count, lambda d, carry: (work(count - d), carry)[1], 0)

    for copy in copies[3:]:
        copy.wait()

    def hot(order_ref):
        return one_hot(lax.broadcasted_iota(jnp.int32, (face, face), 0), order_ref[...])

    west_hot[...] = hot(west_map)
    south_hot[...] = hot(south_map)

    lane = lax.broadcasted_iota(jnp.int32, (1, unknowns), 1)
    flags = [c > 0, c < n_col - 1, a > 0, a < n_row - 1]
    halves = [jnp.where(flag, 0.5, 1.0).astype(F32) for flag in flags]
    weights = jnp.where(
        lane < face,
        halves[0],
        jnp.where(lane < 2 * face, halves[1], jnp.where(lane < 3 * face, halves[2], halves[3])),
    )
    targets = [(a, c + 1), (a, c - 1), (a + 1, c), (a - 1, c)]
    can_send = [flags[1], flags[0], flags[3], flags[2]]

    def face_copy(turn, slot):
        return pltpu.make_async_remote_copy(
            src_ref=face_out.at[turn, slot],
            dst_ref=face_in.at[turn, slot],
            send_sem=face_send.at[turn, slot],
            recv_sem=face_recv.at[turn, slot],
            device_id=targets[slot],
            device_id_type=MESH,
        )

    def near_copy(slot):
        return pltpu.make_async_remote_copy(
            src_ref=near_out,
            dst_ref=near_in.at[slot],
            send_sem=near_send.at[slot],
            recv_sem=near_recv.at[slot],
            device_id=targets[slot],
            device_id_type=MESH,
        )

    def face_fill(turn, values):
        face_out[turn, 0] = values[:, face : 2 * face]
        face_out[turn, 2] = values[:, 3 * face :]
        face_out[turn, 1] = join(dot_nt(split(values[:, :face]), west_hot[...]))
        face_out[turn, 3] = join(dot_nt(split(values[:, 2 * face : 3 * face]), south_hot[...]))

    def when_neighbour(present, work):
        for slot in range(4):
            @pl.when(present[slot])
            def _():
                work(slot)

    def face_finish(turn, values):
        for slot in range(4):
            @pl.when(flags[slot])
            def _():
                face_copy(turn, slot).wait_recv()

            @pl.when(jnp.logical_not(flags[slot]))
            def _():
                face_in[turn, slot] = jnp.zeros(face_in.shape[2:], F32)
        adds = [
            join(dot(split(face_in[turn, 0]), west_hot[...])),
            face_in[turn, 1],
            join(dot(split(face_in[turn, 2]), south_hot[...])),
            face_in[turn, 3],
        ]
        return values + jnp.concatenate(adds, axis=1)

    def column_copy(m):
        return pltpu.make_async_remote_copy(
            src_ref=idx_all.at[spot],
            dst_ref=idx_all.at[spot],
            send_sem=idx_send.at[0],
            recv_sem=idx_recv.at[0],
            device_id=column_mates[m - 1],
            device_id_type=MESH,
        )

    def row_copy(m):
        own = idx_all.at[pl.ds(c * n_row, n_row)]
        return pltpu.make_async_remote_copy(
            src_ref=own,
            dst_ref=own,
            send_sem=idx_send.at[1],
            recv_sem=idx_recv.at[m],
            device_id=(a, cols_of[m] if isinstance(m, int) else flip(c, m, n_col)),
            device_id_type=MESH,
        )

    first = loads[...]
    face_fill(0, first)
    pl.semaphore_wait(barrier, n_row + n_col - 2)
    for mate in column_mates:
        pl.semaphore_signal(entered, inc=1, device_id=mate, device_id_type=MESH)
    when_neighbour(can_send, lambda slot: face_copy(0, slot).start())

    def placed(source):
        place[...] = jnp.full(place.shape, -1, jnp.int32)
        place[:1, :nprim] = source[...]
        base = place[...]
        return base, pltpu.roll(base, half, 1)

    base, rolled = placed(prim_coarse)
    own_coarse = jnp.where(odd == 1, rolled, base)[:1]
    idx_all[spot] = own_coarse
    for m in range(1, n_row):
        column_copy(m).start()
    own_base, own_rolled = placed(prim_local)
    own_ids, numbers = base[:1], own_base[:1]
    depth = lax.broadcasted_iota(jnp.int32, (face, lanes), 0)

    def look_up(table, numbers, offset):
        inside = jnp.logical_and(numbers >= 0, numbers < face)
        table = jnp.broadcast_to(table, (8, face)).astype(F32)
        found = join(dot(split(table), one_hot(depth, numbers)))[:1]
        return jnp.where(inside, found.astype(jnp.int32) + offset, -1)

    to_west = look_up(west_map[...], numbers, face)
    to_south = look_up(south_map[...], numbers - 2 * face, 3 * face)
    row = lax.broadcasted_iota(jnp.int32, near_out.shape, 0)
    near_out[...] = jnp.where(
        row == 0, own_ids, jnp.where(row == 1, numbers, jnp.where(row == 2, to_west, to_south))
    )
    when_neighbour(can_send, lambda slot: near_copy(slot).start())

    own_local = jnp.maximum(own_base, own_rolled)[:1]
    rows_iota = lax.broadcasted_iota(jnp.int32, (unknowns, wide), 0)
    local_hot[...] = one_hot(rows_iota, own_local)

    def all_copy(buffer, kind, m):
        return pltpu.make_async_remote_copy(
            src_ref=buffer.at[spot if kind == RHS else me],
            dst_ref=buffer.at[spot if kind == RHS else me],
            send_sem=all_send.at[kind],
            recv_sem=all_recv.at[kind],
            device_id=peer(m),
            device_id_type=MESH,
        )

    def start(buffer, kind):
        each(lambda m: all_copy(buffer, kind, m).start())

    def await_some(buffer, sent, semaphore):
        slots = buffer.at[pl.ds(0, sent)]
        pltpu.make_async_copy(slots, slots, semaphore).wait()

    def await_all(buffer, semaphore):
        await_some(buffer, count - 1, semaphore)

    def arrive(buffer, kind):
        await_all(buffer, all_recv.at[kind])

    rhs = loads.shape[0]
    lower = lax.broadcasted_iota(jnp.int32, (rhs // 2, wide), 1) < half

    def pack(values):
        return jnp.where(lower, values[: rhs // 2], values[rhs // 2 :])

    square = (rhs, wide)
    stays = (lax.broadcasted_iota(jnp.int32, square, 1) < half) == (
        lax.broadcasted_iota(jnp.int32, square, 0) < rhs // 2
    )

    def unpack(first, second):
        both = jnp.concatenate([first, second], axis=0)
        return jnp.where(stays, both, pltpu.roll(pltpu.roll(both, half, 1), rhs // 2, 0))

    def split_matrix(source, high, low):
        step = 128

        def one(i, carry):
            at = pl.ds(pl.multiple_of(i * step, step), step)
            values = source[at, :]
            top = values.astype(BF16)
            high[at, :] = top
            low[at, :] = (values - top.astype(F32)).astype(BF16)
            return carry

        lax.fori_loop(0, source.shape[0] // step, one, 0)

    chunk = coarse_split.shape[1]
    chunks = coarse_all // chunk
    part = coarse_split.shape[0] // chunks // 2

    def over_chunks(work, carry):
        if chunks <= 8:
            for k in range(chunks):
                carry = work(k, carry)
            return carry
        return lax.fori_loop(0, chunks, work, carry)

    def split_coarse():
        copies[1].wait()
        columns[...] = jnp.zeros(columns.shape, BF16)
        if coarse_rows < part:
            coarse_split[...] = jnp.zeros(coarse_split.shape, BF16)

        def one(k, carry):
            at = k * chunk if isinstance(k, int) else pl.multiple_of(k * chunk, chunk)
            rows = 2 * part * k if isinstance(k, int) else pl.multiple_of(2 * part * k, 2 * part)
            values = coarse_in[:, pl.ds(at, chunk)]
            top = values.astype(BF16)
            coarse_split[pl.ds(rows, coarse_rows), :] = top
            coarse_split[pl.ds(rows + part, coarse_rows), :] = (values - top.astype(F32)).astype(BF16)
            return carry

        over_chunks(one, 0)

    early = c < n_col // 2

    def split_schur():
        copies[2].wait()
        split_matrix(schur_in, schur_hi, schur_lo)

    copies[0].wait()
    split_matrix(factor_in, factor_hi, factor_lo)
    split_coarse()
    pl.when(early)(split_schur)
    right_side = face_finish(0, first)
    scaled = weights * right_side
    val_all[0, spot] = pack(join(dot(split(scaled), local_hot[...])))
    await_some(idx_all, n_row - 1, idx_recv.at[0])
    pl.semaphore_wait(entered, n_row - 1)
    start(val_all.at[0], RHS)
    for m in range(1, n_col):
        row_copy(m).start()

    def apply(high, low, vectors):
        both = split(vectors)
        return join(dot(both, high[...]) + dot(both, low[...]))

    pl.when(jnp.logical_not(early))(split_schur)
    local[...] = apply(factor_hi, factor_lo, scaled)

    def sweep(turn):
        now = local[...]
        inner = scaled - apply(schur_hi, schur_lo, now)
        later = now + apply(factor_hi, factor_lo, inner)
        more = jnp.broadcast_to(elements[...], now.shape) >= turn * ELEM_BASE
        local[...] = jnp.where(more, later, now)

    def last_sweep():
        sweep(MOST_SWEEPS)
        face_fill(1, weights * local[...])
        when_neighbour(can_send, lambda slot: face_copy(1, slot).start())

    for turn in range(2, MOST_SWEEPS):
        sweep(turn)
    pl.when(c >= n_col // 4)(last_sweep)

    group = 16
    span = group // 2 * wide
    small = lax.broadcasted_iota(jnp.int32, (chunk, span), 0).astype(F32).astype(BF16)
    cols_each, blocks = max(1, group // n_row), max(1, n_row // group)

    def one_column(step, carry):
        k = lax.div(step, blocks)
        for i in range(cols_each):
            q = k * cols_each + i

            @pl.when(jnp.logical_and(q > 0, lax.rem(step, blocks) == 0))
            def _():
                row_copy(q).wait_recv()

        s = flip(lax.div(c, cols_each), k, n_col // cols_each) * blocks + lax.rem(step, blocks)
        wanted = jnp.concatenate(
            [
                jnp.maximum(idx_all[group * s + i], idx_all[group * s + i + 1])
                for i in range(0, group, 2)
            ],
            axis=1,
        )
        which = jnp.right_shift(wanted, chunk.bit_length() - 1)
        offset = jnp.bitwise_and(wanted, chunk - 1).astype(F32).astype(BF16)
        picks = jnp.where(small == offset, jnp.ones_like(small), jnp.zeros_like(small))

        if chunks <= 8:
            taken = dot(coarse_split[...], picks)
            acc = jnp.zeros((2 * part, span), F32)
            for k in range(chunks):
                acc = jnp.where(which == k, taken[2 * part * k : 2 * part * (k + 1)], acc)
        else:

            def one_chunk(k, acc):
                rows = pl.ds(pl.multiple_of(2 * part * k, 2 * part), 2 * part)
                return jnp.where(which == k, dot(coarse_split[rows, :], picks), acc)

            acc = lax.fori_loop(0, chunks, one_chunk, jnp.zeros((2 * part, span), F32))
        values = join(acc)
        top = values.astype(BF16)
        at = pl.ds(pl.multiple_of(s * span, span), span)
        columns[:part, at] = top
        columns[half : half + part, at] = (values - top.astype(F32)).astype(BF16)
        return carry

    lax.fori_loop(0, count // group, one_column, 0)

    def gathered(buffer):
        return split(
            jnp.concatenate([unpack(buffer[s], buffer[s + 1]) for s in range(0, count, 2)], axis=1)
        )

    arrive(val_all.at[0], RHS)
    solved = join(dot_nt(gathered(val_all.at[0]), columns[...]))
    solved = solved + pltpu.roll(solved, half, 1)
    val_all[1, me] = pack(solved)
    start(val_all.at[1], SOL)

    pl.when(c < n_col // 4)(last_sweep)

    for slot in range(4):
        @pl.when(flags[slot])
        def _():
            near_copy(slot).wait_recv()

        @pl.when(jnp.logical_not(flags[slot]))
        def _():
            near_in[slot] = jnp.full(near_in.shape[1:], -1, jnp.int32)

    def inverse(order_hot):
        order = lax.broadcasted_iota(jnp.int32, (8, face), 1).astype(F32)
        return join(dot_nt(split(order), order_hot[...]))[:1]

    def in_turn(rows):
        joined = None
        for i, row in enumerate(rows):
            wide_place[...] = jnp.full(wide_place.shape, -1, jnp.int32)
            wide_place[:1, :lanes] = row
            row = wide_place[...]
            row = pltpu.roll(row, i * nprim, 1) if i else row
            joined = row if joined is None else jnp.maximum(joined, row)
        return joined[:1]

    west, east, south, north = [near_in[slot] for slot in range(4)]
    target = in_turn(
        [
            numbers,
            look_up(inverse(west_hot), west[1:2] - face, 0),
            east[2:3],
            look_up(inverse(south_hot), south[1:2] - 3 * face, 2 * face),
            north[3:4],
        ]
    )
    wanted_coarse = in_turn([own_ids] + [near[:1] for near in (west, east, south, north)])
    target = jnp.broadcast_to(target.astype(F32), (8, five)).T[:, :1].astype(jnp.int32)
    place_hot[...] = jnp.where(
        lax.broadcasted_iota(jnp.int32, (five, unknowns), 1) == target, weights, 0.0
    ).astype(BF16)
    spread = dot(place_hot[...], schur_hi[...]) + dot(place_hot[...], schur_lo[...])
    top = spread.astype(BF16)
    spread_hi[...] = top
    spread_lo[...] = (spread - top.astype(F32)).astype(BF16)

    at = lax.broadcasted_iota(jnp.int32, (wide, five), 0)
    upper = (at >= half).astype(jnp.int32)
    number = upper * coarse_rows + at - upper * half
    number = jnp.where(at - upper * half < coarse_rows, number, -2 * coarse_all)

    def one_pick(s, carry):
        coarse_hot[pl.ds(pl.multiple_of(s * wide, wide), wide), :] = one_hot(
            number, wanted_coarse - s * 2 * coarse_rows
        )
        return carry

    lax.fori_loop(0, count // 2, one_pick, 0)
    before = face_finish(1, weights * local[...])
    image_before = apply(schur_hi, schur_lo, before)

    def lane_sum(values):
        return jnp.sum(values, axis=1, keepdims=True)

    arrive(val_all.at[1], SOL)
    read = split(join(dot(gathered(val_all.at[1]), coarse_hot[...])))
    precond = before + join(dot(read, place_hot[...]))
    image = image_before + join(dot(read, spread_hi[...]) + dot(read, spread_lo[...]))
    rz = lane_sum(scaled * precond)
    pq = lane_sum(precond * image)
    sum_lane = lax.broadcasted_iota(jnp.int32, (rhs, 128), 1)
    sum_case = lax.broadcasted_iota(jnp.int32, (rhs, 128), 0)
    upper_lane, lower_lane = sum_lane == sum_case + rhs, sum_lane == sum_case
    laid = jnp.where(lower_lane, rz, 0.0) + jnp.where(upper_lane, pq, 0.0)
    sum_all[me] = jnp.sum(laid, axis=0, keepdims=True)
    start(sum_all, SUM)
    face_fill(2, image)
    when_neighbour(can_send, lambda slot: face_copy(2, slot).start())
    direction[...] = precond
    loads_out[...] = right_side
    await_some(idx_all, n_row - 1, idx_send.at[0])
    await_some(idx_all, n_row * (n_col - 1), idx_send.at[1])
    await_all(val_all.at[0], all_send.at[RHS])
    await_all(val_all.at[1], all_send.at[SOL])
    for turn in range(2):
        when_neighbour(can_send, lambda slot: face_copy(turn, slot).wait_send())
    when_neighbour(can_send, lambda slot: near_copy(slot).wait_send())
    image_out[...] = face_finish(2, image)
    arrive(sum_all, SUM)
    parts = [sum_all[i] for i in range(count)]
    while len(parts) > 1:
        parts = [x + y for x, y in zip(parts[::2], parts[1::2])]
    sums = jnp.broadcast_to(parts[0], (rhs, 128))
    alpha = lane_sum(jnp.where(lower_lane, sums, 0.0)) / lane_sum(jnp.where(upper_lane, sums, 0.0))
    alpha_out[...] = jnp.broadcast_to(alpha, alpha_out.shape)
    await_all(sum_all, all_send.at[SUM])
    when_neighbour(can_send, lambda slot: face_copy(2, slot).wait_send())


def up(n, to):
    return -(-n // to) * to


def body(
    n_row, n_col, loads, schur, factor, coarse_inverse, elements, west_map, south_map,
    prim_local, prim_coarse,
):
    vectors = loads[0, 0].T
    rhs, unknowns = vectors.shape
    face = unknowns // 4
    coarse_rows, coarse_all = coarse_inverse.shape
    nprim = prim_local.shape[2]
    wide = 2 * up(max(nprim, coarse_rows), 64)
    count = n_row * n_col
    lanes, five = wide, max(wide, up(5 * nprim, 128))
    vmem = pl.BlockSpec(memory_space=pltpu.VMEM)
    hbm = pl.BlockSpec(memory_space=pl.ANY)
    dma = pltpu.SemaphoreType.DMA
    out = pltpu.VMEM(vectors.shape, F32)
    direction, image, right_side, alpha = pl.pallas_call(
        functools.partial(kernel, n_row, n_col),
        out_shape=(out, out, out, out),
        in_specs=[hbm] * 9,
        out_specs=(vmem, vmem, vmem, vmem),
        scratch_shapes=[
            pltpu.VMEM(vectors.shape, F32),
            pltpu.VMEM((1, 1), jnp.int32),
            pltpu.VMEM((1, face), jnp.int32),
            pltpu.VMEM((1, face), jnp.int32),
            pltpu.VMEM((1, nprim), jnp.int32),
            pltpu.VMEM((1, nprim), jnp.int32),
            pltpu.VMEM((unknowns, unknowns), F32),
            pltpu.VMEM((unknowns, unknowns), F32),
            pltpu.VMEM((coarse_rows, coarse_all), F32),
            pltpu.VMEM((unknowns, unknowns), BF16),
            pltpu.VMEM((unknowns, unknowns), BF16),
            pltpu.VMEM((unknowns, unknowns), BF16),
            pltpu.VMEM((unknowns, unknowns), BF16),
            pltpu.VMEM((coarse_all // face * 2 * up(coarse_rows, 16), face), BF16),
            pltpu.VMEM((wide, count // 2 * wide), BF16),
            pltpu.VMEM((face, face), BF16),
            pltpu.VMEM((face, face), BF16),
            pltpu.VMEM((unknowns, wide), BF16),
            pltpu.VMEM((count // 2 * wide, five), BF16),
            pltpu.VMEM((five, unknowns), BF16),
            pltpu.VMEM((five, unknowns), BF16),
            pltpu.VMEM((five, unknowns), BF16),
            pltpu.VMEM(vectors.shape, F32),
            pltpu.VMEM((8, wide), jnp.int32),
            pltpu.VMEM((8, five), jnp.int32),
            pltpu.VMEM((count, 1, wide), jnp.int32),
            pltpu.VMEM((2, count, rhs // 2, wide), F32),
            pltpu.VMEM((count, 1, 128), F32),
            pltpu.VMEM((3, 4, rhs, face), F32),
            pltpu.VMEM((3, 4, rhs, face), F32),
            pltpu.VMEM((8, lanes), jnp.int32),
            pltpu.VMEM((4, 8, lanes), jnp.int32),
            dma((9,)),
            dma((3, 4)),
            dma((3, 4)),
            dma((4,)),
            dma((4,)),
            dma((2,)),
            dma((n_col,)),
            dma((3,)),
            dma((3,)),
            pltpu.SemaphoreType.REGULAR,
        ],
        compiler_params=pltpu.CompilerParams(collective_id=0, has_side_effects=True),
    )(
        vectors, schur[0, 0], factor[0, 0], coarse_inverse, elements,
        west_map[0], south_map[0], prim_local[0], prim_coarse[0],
    )
    solution = alpha * direction
    residual = right_side - alpha * image
    return solution.T[None, None], residual.T[None, None]


def solution(mesh):
    placed = (
        P("row", "col", None, None),
        P("row", "col", None, None),
        P("row", "col", None, None),
        P(("row", "col"), None),
        P("row", "col"),
        P("row", "col", None),
        P("row", "col", None),
        P("row", "col", None),
        P("row", "col", None),
    )
    return jax.shard_map(
        functools.partial(body, mesh.shape["row"], mesh.shape["col"]),
        mesh=mesh,
        in_specs=placed,
        out_specs=(P("row", "col", None, None), P("row", "col", None, None)),
        check_vma=False,
    )
```
